32 devices in a mesh: groups: 2 (over y), ctx: 16 (over z, x, core).
Axes of the slice: x: 2, y: 2, z: 4, core: 2. Of those that a mesh axis runs over, the one named last changes fastest.
Arguments:
- child_q: bfloat16 [32, 128, 4096], P(('groups', 'ctx')), parts along dimension 0, may hold values from -8 to 8
- child_kv: bfloat16 [32, 128, 2, 512], P(('groups', 'ctx')), parts along dimension 0, may hold values from -12 to 12
- prompt_kv: bfloat16 [128, 2, 512], P(('groups', 'ctx')), parts along dimension 0, may hold values from -12 to 12
- parent_kv: bfloat16 [256, 2, 2, 512], P(('groups', 'ctx')), parts along dimension 0, may hold values from -12 to 12
- fork_list: int32 [32], P('groups'), parts along dimension 0, may hold values from 0 to 1
- owner_map: int32 [4, 16], P('groups'), parts along dimension 0, may hold values from 0 to 15, each once within a row
- lengths: int32 [4], P('groups'), parts along dimension 0, may hold values from 1 to 128, as said below
Outputs:
- child_out: bfloat16 [32, 128, 4096], P(('groups', 'ctx')), parts along dimension 0
The draws below stay inside these ranges and needn't reach their ends.
There are 2 independent parts, one for each index of `groups`. The reference program is written for one: setup_inputs(seed, part) draws one part's arguments, and reference() takes and returns one part's arrays. A program takes and returns all parts, laid end to end along the dimension named above; each array names one. Nothing has to cross between parts.
Inputs may be any that keep to these rules, and one draw needn't show every extreme that they name: `lengths`: some parent has all 128 positions valid.
All inputs are finite; a program needn't handle non-finite values.
Results may differ from the reference program's by a relative error of at most 0.0032.
Values may be sent and summed in bfloat16 or wider, within the bound.
No kernel may reach another device: no remote copies, remote signals or barrier semaphores. Data moves between devices by JAX's collectives and lax.ppermute only.
A program may use at most 64 MiB of HBM per device.

```python
import math
import jax
import jax.numpy as jnp
import numpy as np
from jax import lax

HQ = 32
KVH = 4
HD = 128
SPAN = 128
SEGD = 8
CHILDREN = 16
PARENTS = 2
PROMPT = 64
SEG = 128


def kv_field(key, shape, salt):
    field = jnp.clip(2.0 * jax.random.normal(jax.random.fold_in(key, salt), shape, jnp.float32), -12.0, 12.0)
    return field.astype(jnp.bfloat16)


def draw_child_q(key, part):
    shape = (CHILDREN, SPAN, HQ * HD)
    field = jnp.clip(jax.random.normal(jax.random.fold_in(key, 11), shape, jnp.float32), -6.0, 6.0)
    return field.astype(jnp.bfloat16)


def draw_child_kv(key, part):
    return kv_field(key, (CHILDREN, SPAN, 2, KVH * HD), 23)


def draw_prompt_kv(key, part):
    return kv_field(key, (PROMPT, 2, KVH * HD), 29)


def draw_parent_kv(key, part):
    return kv_field(key, (SEG, PARENTS, 2, KVH * HD), 41)


def draw_lengths(key, part):
    base = jax.random.randint(jax.random.fold_in(key, 31), (PARENTS,), 1, SEG + 1)
    chosen = jax.random.randint(jax.random.fold_in(key, 37), (), 0, PARENTS)
    return jnp.where(jnp.arange(PARENTS) == chosen, SEG, base).astype(jnp.int32)


def set_ends(entries, key, least, high):
    place = [jax.random.randint(jax.random.fold_in(key, axis), (), 0, length) for axis, length in enumerate(entries.shape)]
    widest = entries.shape.index(max(entries.shape))
    neighbour = place[:widest] + [(place[widest] + 1) % entries.shape[widest]] + place[widest + 1:]
    return entries.at[tuple(place)].set(least).at[tuple(neighbour)].set(high)


def rank_bounds(amount, lean):
    weights = [(1 << 20) // math.isqrt(standing ** lean) + 1 for standing in range(1, amount + 1)]
    spread = 1 + sum(weights) // (1 << 30)
    return np.cumsum(np.array([max(1, weight // spread) for weight in weights]))


def ranked(key, shape, number_of, slope):
    listing = rank_bounds(number_of, slope)
    ticket = jax.random.randint(jax.random.fold_in(key, 1), shape, 0, int(listing[number_of - 1]))
    grade = jnp.searchsorted(jnp.asarray(listing, jnp.int32), ticket, side="right")
    return jax.random.permutation(jax.random.fold_in(key, 2), number_of)[grade].astype(jnp.int32)


def setup_inputs(seed: int = 0, part: int = 0) -> dict:
    seeds = jax.random.split(jax.random.key(seed), 8)
    part_splits = jax.random.split(jax.random.fold_in(seeds[7], part), 8)
    return {
        "child_q": draw_child_q(jax.random.fold_in(jax.random.fold_in(seeds[7], part), 71), part),
        "child_kv": draw_child_kv(jax.random.fold_in(jax.random.fold_in(seeds[7], part), 71), part),
        "prompt_kv": draw_prompt_kv(jax.random.fold_in(jax.random.fold_in(seeds[7], part), 71), part),
        "parent_kv": draw_parent_kv(jax.random.fold_in(jax.random.fold_in(seeds[7], part), 71), part),
        "fork_list": set_ends(ranked(part_splits[4], (CHILDREN,), PARENTS, 2), jax.random.fold_in(part_splits[4], 3), 0, PARENTS - 1).astype(jnp.int32),
        "owner_map": jax.vmap(lambda own: jax.random.permutation(own, CHILDREN))(jax.random.split(part_splits[5], PARENTS)).reshape((PARENTS, CHILDREN)).astype(jnp.int32),
        "lengths": draw_lengths(jax.random.fold_in(jax.random.fold_in(seeds[7], part), 71), part),
    }


def level_part(queries, key_rows, value_rows, allowed):
    scaling = queries.shape[1] ** -0.5
    scores = jnp.dot(queries.astype(jnp.float32), key_rows.astype(jnp.float32).T, precision=lax.Precision.HIGHEST) * scaling
    if allowed is not None:
        scores = jnp.where(allowed, scores, -jnp.inf)
    highest = jnp.max(scores, axis=1)
    weights = jnp.exp(scores - highest[:, None])
    if allowed is not None:
        weights = jnp.where(allowed, weights, 0.0)
    weights = lax.optimization_barrier(weights.astype(jnp.bfloat16))
    widened = weights.astype(jnp.float32)
    totals = jnp.sum(widened, axis=1)
    weighted = jnp.dot(widened, value_rows.astype(jnp.float32), precision=lax.Precision.HIGHEST)
    return highest, totals, weighted


def merge_levels(former, latter):
    highest = jnp.maximum(former[0], latter[0])
    weight_one = jnp.exp(former[0] - highest)
    weight_two = jnp.exp(latter[0] - highest)
    totals = former[1] * weight_one + latter[1] * weight_two
    weighted = former[2] * weight_one[:, None] + latter[2] * weight_two[:, None]
    return highest, totals, weighted


def reference(child_q, child_kv, prompt_kv, parent_kv, fork_list, owner_map, lengths):
    group_size = HQ // KVH
    places = jnp.arange(CHILDREN, dtype=jnp.int32)
    query_time = jnp.arange(SPAN * group_size, dtype=jnp.int32) // group_size
    causal = jnp.arange(SPAN, dtype=jnp.int32)[None, :] <= query_time[:, None]

    def one_child(child):
        queries = child_q[child]
        own_rows = child_kv[child]
        parent = fork_list[child]
        segment = jnp.take(parent_kv, parent, axis=1)
        owner_row = owner_map[parent]
        matches = owner_row[None, :] == places[:, None]
        pieces = jnp.sum(jnp.where(matches, places[None, :], 0), axis=1)
        positions = (pieces[:, None] * SEGD + jnp.arange(SEGD, dtype=jnp.int32)[None, :]).reshape(SEG)
        allowed = (positions < lengths[parent])[None, :]
        results = []
        for kv_head in range(KVH):
            low = kv_head * HD
            high = low + HD
            head_queries = queries[:, kv_head * group_size * HD:(kv_head + 1) * group_size * HD].reshape(SPAN * group_size, HD)
            prompt_stats = level_part(head_queries, prompt_kv[:, 0, low:high], prompt_kv[:, 1, low:high], None)
            parent_stats = level_part(head_queries, segment[:, 0, low:high], segment[:, 1, low:high], allowed)
            own_stats = level_part(head_queries, own_rows[:, 0, low:high], own_rows[:, 1, low:high], causal)
            merged = merge_levels(merge_levels(prompt_stats, parent_stats), own_stats)
            results.append((merged[2] / merged[1][:, None]).reshape(SPAN, group_size * HD))
        return jnp.concatenate(results, axis=1).astype(jnp.bfloat16)

    return lax.map(one_child, jnp.arange(CHILDREN, dtype=jnp.int32))
```

```python
import functools

import jax
import jax.numpy as jnp
from jax import lax
from jax.experimental import pallas as pl
from jax.experimental.pallas import tpu as pltpu
from jax.sharding import PartitionSpec as P

HD = 128
LOG2E = 1.4426950408889634
F32 = jnp.float32
BF16 = jnp.bfloat16


def pack_kernel(fork_ref, prompt_ref, parent_ref, send_ref, table_ref):
    prompt = prompt_ref[...].astype(F32)
    shared = [prompt[:, 0, :], prompt[:, 1, :]]
    for p in range(parent_ref.shape[1]):
        piece = parent_ref[:, p].astype(F32)
        table_ref[p] = jnp.concatenate([piece[:, 0, :], piece[:, 1, :], *shared], axis=0).astype(BF16)

    def place(d, carry):
        send_ref[d] = table_ref[fork_ref[d]]
        return carry

    lax.fori_loop(0, send_ref.shape[0], place, 0, unroll=min(8, send_ref.shape[0]))


def mask_kernel(seg_rows, prompt_rows, fork_ref, owner_ref, lengths_ref, bias_ref):
    blocks = owner_ref.shape[1]
    device = lax.axis_index("ctx")
    parent = fork_ref[device]
    lane = lax.broadcasted_iota(jnp.int32, (8, blocks * seg_rows), 1)
    block, row = lane // seg_rows, lane % seg_rows

    def step(j, position):
        return jnp.where(block == owner_ref[parent, j], j * seg_rows + row, position)

    position = lax.fori_loop(0, blocks, step, jnp.zeros_like(lane), unroll=min(8, blocks))
    bias_ref[:, : blocks * seg_rows] = jnp.where(position < lengths_ref[parent], 0.0, -jnp.inf)
    tile = lax.broadcasted_iota(jnp.int32, (8, blocks * 2 * prompt_rows), 1)
    bias_ref[:, blocks * seg_rows :] = jnp.where(tile % (2 * prompt_rows) < prompt_rows, 0.0, -jnp.inf)


def attend_kernel(seg_rows, prompt_rows, q_ref, own_ref, got_ref, bias_ref, out_ref):
    span = q_ref.shape[1]
    group = q_ref.shape[2] // HD
    n = got_ref.shape[0]
    got = got_ref[...].astype(F32)
    par_k = got[:, :seg_rows].reshape(n * seg_rows, HD)
    par_v = got[:, seg_rows : 2 * seg_rows].reshape(n * seg_rows, HD)
    pro = got[:, 2 * seg_rows :].reshape(n * 2 * prompt_rows, HD)
    pro_v = pltpu.roll(pro, pro.shape[0] - prompt_rows, 0)
    own = own_ref[...].astype(F32)
    keys = jnp.concatenate([par_k, pro, own[:, 0, :]], axis=0).astype(BF16)
    values = jnp.concatenate([par_v, pro_v, own[:, 1, :]], axis=0)
    values = jnp.concatenate([values, jnp.ones_like(values)], axis=1).astype(BF16)
    far = n * (seg_rows + 2 * prompt_rows)
    factor = LOG2E * HD**-0.5
    row = lax.broadcasted_iota(jnp.int32, (span, span), 0)
    column = lax.broadcasted_iota(jnp.int32, (span, span), 1)
    causal = jnp.where(column <= row, 0.0, -jnp.inf)
    bias = jnp.concatenate([jnp.broadcast_to(bias_ref[0:1, :], (span, far)), causal], axis=1)
    for h in range(group):
        query = q_ref[0, :, h * HD : (h + 1) * HD]
        scores = lax.dot_general(query, keys, (((1,), (1,)), ((), ())), preferred_element_type=F32)
        scores = scores * factor + bias
        highest = jnp.max(scores, axis=1, keepdims=True)
        weights = jnp.exp2(scores - highest).astype(BF16)
        both = jnp.dot(weights, values, preferred_element_type=F32)
        out_ref[0, :, h * HD : (h + 1) * HD] = (both[:, :HD] / both[:, HD:]).astype(BF16)


def body(child_q, child_kv, prompt_kv, parent_kv, fork_list, owner_map, lengths):
    n = lax.axis_size("ctx")
    seg_rows, prompt_rows = parent_kv.shape[0], prompt_kv.shape[0]
    span, width = child_kv.shape[1], child_kv.shape[3]
    columns = child_q.shape[2]
    kv_heads = width // HD
    group_width = columns // kv_heads
    chunk = 2 * (seg_rows + prompt_rows)
    vmem = pl.BlockSpec(memory_space=pltpu.VMEM)
    smem = pl.BlockSpec(memory_space=pltpu.SMEM)
    send = pl.pallas_call(
        pack_kernel,
        out_shape=jax.ShapeDtypeStruct((n, chunk, width), BF16),
        in_specs=[smem, vmem, vmem],
        out_specs=vmem,
        scratch_shapes=[pltpu.VMEM((parent_kv.shape[1], chunk, width), BF16)],
        name="pack",
    )(fork_list, prompt_kv, parent_kv)
    got = lax.all_to_all(send, "ctx", split_axis=0, concat_axis=0, tiled=True)
    far = n * (seg_rows + 2 * prompt_rows)
    bias = pl.pallas_call(
        functools.partial(mask_kernel, seg_rows, prompt_rows),
        out_shape=jax.ShapeDtypeStruct((8, far), F32),
        in_specs=[smem, smem, smem],
        out_specs=vmem,
        name="mask",
    )(fork_list, owner_map, lengths)
    return pl.pallas_call(
        functools.partial(attend_kernel, seg_rows, prompt_rows),
        out_shape=jax.ShapeDtypeStruct(child_q.shape, BF16),
        grid=(kv_heads,),
        in_specs=[
            pl.BlockSpec((1, span, group_width), lambda g: (0, 0, g)),
            pl.BlockSpec((span, 2, HD), lambda g: (0, 0, g)),
            pl.BlockSpec((n, chunk, HD), lambda g: (0, 0, g)),
            pl.BlockSpec((8, far), lambda g: (0, 0)),
        ],
        out_specs=pl.BlockSpec((1, span, group_width), lambda g: (0, 0, g)),
        name="attend",
    )(child_q, child_kv[0], got, bias)


def solution(mesh):
    placed = (
        P(("groups", "ctx"), None, None),
        P(("groups", "ctx"), None, None, None),
        P(("groups", "ctx"), None, None),
        P(("groups", "ctx"), None, None, None),
        P("groups"),
        P("groups", None),
        P("groups"),
    )
    return jax.shard_map(
        body,
        mesh=mesh,
        in_specs=placed,
        out_specs=P(("groups", "ctx"), None, None),
        check_vma=False,
    )
```

```python
import functools

import jax
import jax.numpy as jnp
from jax import lax
from jax.experimental import pallas as pl
from jax.experimental.pallas import tpu as pltpu
from jax.sharding import PartitionSpec as P

HD = 128
LOG2E = 1.4426950408889634
F32 = jnp.float32
BF16 = jnp.bfloat16
VMEM = pl.BlockSpec(memory_space=pltpu.VMEM)
SMEM = pl.BlockSpec(memory_space=pltpu.SMEM)
ANY = pl.BlockSpec(memory_space=pl.ANY)


def limit(mib):
    return pltpu.CompilerParams(vmem_limit_bytes=mib << 20)


def shard_rows(prompt_ref, parent_ref):
    prompt = prompt_ref[...].astype(F32)
    rows = []
    for p in range(parent_ref.shape[1]):
        piece = parent_ref[:, p].astype(F32)
        rows += [piece[:, 0, :], piece[:, 1, :]]
    return rows, [prompt[:, 0, :], prompt[:, 1, :]]


def shard_kernel(prompt_ref, parent_ref, out_ref):
    pieces, shared = shard_rows(prompt_ref, parent_ref)
    out_ref[...] = jnp.concatenate(pieces + shared, axis=0).astype(BF16)


def pack_kernel(fork_ref, prompt_ref, parent_ref, send_ref, table_ref):
    pieces, shared = shard_rows(prompt_ref, parent_ref)
    for p in range(parent_ref.shape[1]):
        table_ref[p] = jnp.concatenate(pieces[2 * p : 2 * p + 2] + shared, axis=0).astype(BF16)

    def place(d, carry):
        send_ref[d] = table_ref[fork_ref[d]]
        return carry

    lax.fori_loop(0, send_ref.shape[0], place, 0, unroll=min(8, send_ref.shape[0]))


def mask_kernel(seg_rows, prompt_rows, offsets, fork_ref, owner_ref, lengths_ref, bias_ref):
    n = owner_ref.shape[1]
    device = lax.axis_index("ctx")
    parent = fork_ref[device]
    lane = lax.broadcasted_iota(jnp.int32, (8, n * seg_rows), 1)
    block, row = lane // seg_rows, lane % seg_rows
    if offsets is not None:
        place = block
        block = jnp.zeros_like(lane)
        for k in range(n):
            owner = device ^ jnp.where(device % 2 == 0, offsets[0][k], offsets[1][k])
            block = jnp.where(place == k, owner, block)

    def step(j, position):
        return jnp.where(block == owner_ref[parent, j], j * seg_rows + row, position)

    position = lax.fori_loop(0, n, step, jnp.zeros_like(lane), unroll=min(16, n))
    bias_ref[:, : n * seg_rows] = jnp.where(position < lengths_ref[parent], 0.0, -jnp.inf)
    tile = lax.broadcasted_iota(jnp.int32, (8, n * 2 * prompt_rows), 1)
    bias_ref[:, n * seg_rows :] = jnp.where(tile % (2 * prompt_rows) < prompt_rows, 0.0, -jnp.inf)


def attend_kernel(seg_rows, prompt_rows, one_parent, fork_ref, q_ref, own_ref, bias_ref, *refs):
    *shards, out_ref, stage, sems = refs
    span, columns = q_ref.shape[1:]
    kv_heads = own_ref.shape[2] // HD
    group = columns // HD // kv_heads
    first = 0 if one_parent else fork_ref[lax.axis_index("ctx")] * (2 * seg_rows)
    row = lax.broadcasted_iota(jnp.int32, (span, span), 0)
    column = lax.broadcasted_iota(jnp.int32, (span, span), 1)
    causal = jnp.where(column <= row, 0.0, -jnp.inf)
    bias = jnp.concatenate([jnp.broadcast_to(bias_ref[0:1, :], (span, bias_ref.shape[1])), causal], axis=1)
    factor = LOG2E * HD**-0.5

    def gathered(start, size, g):
        parts = [r[:, pl.ds(start, size), g * HD : (g + 1) * HD].astype(F32).reshape(-1, HD) for r in shards]
        return jnp.concatenate(parts, axis=0)

    copies = []
    for g in range(kv_heads):
        own = own_ref[:, :, g * HD : (g + 1) * HD].astype(F32)
        prompt = gathered(shards[0].shape[1] - 2 * prompt_rows, 2 * prompt_rows, g)
        prompt_values = pltpu.roll(prompt, prompt.shape[0] - prompt_rows, 0)
        parent_keys = gathered(pl.multiple_of(first, 8), seg_rows, g)
        parent_values = gathered(pl.multiple_of(first + seg_rows, 8), seg_rows, g)
        keys = jnp.concatenate([parent_keys, prompt, own[:, 0, :]], axis=0).astype(BF16)
        values = jnp.concatenate([parent_values, prompt_values, own[:, 1, :]], axis=0)
        values = jnp.concatenate([values, jnp.ones_like(values)], axis=1).astype(BF16)
        for h in range(g * group, (g + 1) * group):
            query = q_ref[0, :, h * HD : (h + 1) * HD]
            scores = lax.dot_general(query, keys, (((1,), (1,)), ((), ())), preferred_element_type=F32)
            scores = scores * factor + bias
            highest = jnp.max(scores, axis=1, keepdims=True)
            weights = jnp.exp2(scores - highest).astype(BF16)
            both = jnp.dot(weights, values, preferred_element_type=F32)
            stage[:, h * HD : (h + 1) * HD] = (both[:, :HD] / both[:, HD:]).astype(BF16)
        part = pl.ds(g * group * HD, group * HD)
        copies.append(pltpu.make_async_copy(stage.at[:, part], out_ref.at[0, :, part], sems.at[g]))
        copies[-1].start()
    for copy in copies:
        copy.wait()


def permute(x, target, n):
    return lax.ppermute(x, "ctx", [(i, target(i)) for i in range(n)])


def gather_shards(shard, n):
    chips = n // 2
    far, near = 2 * (chips - 2), 2
    first = permute(shard, lambda i: i ^ far, n)
    mate = permute(shard, lambda i: i ^ 1, n)
    side = permute(shard, lambda i: i ^ near, n)
    both = jnp.concatenate([shard, mate], axis=0)
    pairs = range(chips // 2 - 2, 0, -1)
    wide = [permute(both, lambda i, j=j: i ^ (2 * (2 * j + i % 2)), n) for j in pairs]
    passed = permute(first, lambda i: i ^ near, n)
    mine = jnp.concatenate([first, passed, side, *wide], axis=0)
    theirs = permute(mine, lambda i: i ^ 1, n)
    got = [[far, far ^ near, near], [far, far ^ near, near]]
    for j in pairs:
        for core in range(2):
            d = 2 * (2 * j + core)
            got[core] += [d, d ^ 1]
    offsets = [[0, 1, *got[core], *[o ^ 1 for o in got[1 - core]]] for core in range(2)]
    return [shard, mate, mine, theirs], offsets


def body(child_q, child_kv, prompt_kv, parent_kv, fork_list, owner_map, lengths):
    n = lax.axis_size("ctx")
    seg_rows, prompt_rows = parent_kv.shape[0], prompt_kv.shape[0]
    parents = parent_kv.shape[1]
    span, width = child_kv.shape[1], child_kv.shape[3]
    kv_heads = width // HD
    gather = n >= 8 and n & (n - 1) == 0 and parents * seg_rows + prompt_rows <= 2 * (seg_rows + prompt_rows)
    if gather:
        rows = 2 * (parents * seg_rows + prompt_rows)
        shard = pl.pallas_call(
            shard_kernel,
            out_shape=jax.ShapeDtypeStruct((rows, width), BF16),
            in_specs=[VMEM, VMEM],
            out_specs=VMEM,
            compiler_params=limit(2),
            name="shard",
        )(prompt_kv, parent_kv)
        shards, offsets = gather_shards(shard, n)
    else:
        rows = 2 * (seg_rows + prompt_rows)
        send = pl.pallas_call(
            pack_kernel,
            out_shape=jax.ShapeDtypeStruct((n, rows, width), BF16),
            in_specs=[SMEM, VMEM, VMEM],
            out_specs=VMEM,
            scratch_shapes=[pltpu.VMEM((parents, rows, width), BF16)],
            name="pack",
        )(fork_list, prompt_kv, parent_kv)
        shards, offsets = [lax.all_to_all(send, "ctx", split_axis=0, concat_axis=0, tiled=True)], None
    shards = [s.reshape(-1, rows, width) for s in shards]
    bias = pl.pallas_call(
        functools.partial(mask_kernel, seg_rows, prompt_rows, offsets),
        out_shape=jax.ShapeDtypeStruct((8, n * (seg_rows + 2 * prompt_rows)), F32),
        in_specs=[SMEM, SMEM, SMEM],
        out_specs=VMEM,
        compiler_params=limit(2),
        name="mask",
    )(fork_list, owner_map, lengths)
    return pl.pallas_call(
        functools.partial(attend_kernel, seg_rows, prompt_rows, not gather),
        out_shape=jax.ShapeDtypeStruct(child_q.shape, BF16),
        in_specs=[SMEM, VMEM, VMEM, VMEM] + [VMEM] * len(shards),
        out_specs=ANY,
        scratch_shapes=[pltpu.VMEM(child_q.shape[1:], BF16), pltpu.SemaphoreType.DMA((kv_heads,))],
        compiler_params=limit(16 if gather else 48),
        name="attend",
    )(fork_list, child_q, child_kv[0], bias, *shards)


def solution(mesh):
    placed = (
        P(("groups", "ctx"), None, None),
        P(("groups", "ctx"), None, None, None),
        P(("groups", "ctx"), None, None),
        P(("groups", "ctx"), None, None, None),
        P("groups"),
        P("groups", None),
        P("groups"),
    )
    return jax.shard_map(
        body,
        mesh=mesh,
        in_specs=placed,
        out_specs=P(("groups", "ctx"), None, None),
        check_vma=False,
    )
```

```python
import functools

import jax
import jax.numpy as jnp
from jax import lax
from jax.experimental import pallas as pl
from jax.experimental.pallas import tpu as pltpu
from jax.sharding import PartitionSpec as P

HD = 128
LOG2E = 1.4426950408889634
F32 = jnp.float32
BF16 = jnp.bfloat16
PAIR = 2
VMEM = pl.BlockSpec(memory_space=pltpu.VMEM)
SMEM = pl.BlockSpec(memory_space=pltpu.SMEM)
HBM = pl.BlockSpec(memory_space=pltpu.HBM)


def in_hbm(*arrays):
    return [pltpu.with_memory_space_constraint(x, pltpu.HBM) for x in arrays]


def limit(mib):
    return pltpu.CompilerParams(vmem_limit_bytes=mib << 20)


def shard_rows(prompt_ref, parent_ref):
    prompt = prompt_ref[...].astype(F32)
    rows = []
    for p in range(parent_ref.shape[1]):
        piece = parent_ref[:, p].astype(F32)
        rows += [piece[:, 0, :], piece[:, 1, :]]
    return rows, [prompt[:, 0, :], prompt[:, 1, :]]


def shard_kernel(prompt_hbm, parent_hbm, out_ref, prompt_ref, parent_ref, sems):
    copies = [
        pltpu.make_async_copy(parent_hbm, parent_ref, sems.at[0]),
        pltpu.make_async_copy(prompt_hbm, prompt_ref, sems.at[1]),
    ]
    for copy in copies:
        copy.start()
    for copy in copies:
        copy.wait()
    pieces, shared = shard_rows(prompt_ref, parent_ref)
    out_ref[...] = jnp.concatenate(pieces + shared, axis=0).astype(BF16)


def pack_kernel(fork_ref, prompt_ref, parent_ref, send_ref, table_ref):
    pieces, shared = shard_rows(prompt_ref, parent_ref)
    for p in range(parent_ref.shape[1]):
        table_ref[p] = jnp.concatenate(pieces[2 * p : 2 * p + 2] + shared, axis=0).astype(BF16)

    def place(d, carry):
        send_ref[d] = table_ref[fork_ref[d]]
        return carry

    lax.fori_loop(0, send_ref.shape[0], place, 0, unroll=min(8, send_ref.shape[0]))


def valid_keys(key, span, seg_rows, prompt_rows, counts, offsets, fork_ref, owner_ref, lengths_ref):
    n = owner_ref.shape[1]
    device = lax.axis_index("ctx")
    parent = fork_ref[device]
    place, row = jnp.full_like(key, -1), jnp.zeros_like(key)
    prompt = key < 0
    start, shard = span, 0
    for count in counts:
        slot = key - start
        here = (slot >= 0) & (slot < count * seg_rows)
        place = jnp.where(here, shard + slot // seg_rows, place)
        row = jnp.where(here, slot % seg_rows, row)
        slot = slot - count * seg_rows
        here = (slot >= 0) & (slot < count * 2 * prompt_rows)
        prompt = prompt | (here & (slot % (2 * prompt_rows) < prompt_rows))
        start += count * (seg_rows + 2 * prompt_rows)
        shard += count
    block = place
    if offsets is not None:
        block = jnp.full_like(key, -1)
        for k in range(n):
            owner = device ^ jnp.where(device % 2 == 0, offsets[0][k], offsets[1][k])
            block = jnp.where(place == k, owner, block)

    def step(j, position):
        return jnp.where(block == owner_ref[parent, j], j * seg_rows + row, position)

    far = jnp.full_like(key, n * seg_rows)
    position = lax.fori_loop(0, n, step, far, unroll=min(16, n))
    return (key < span) | prompt | (position < lengths_ref[parent])


def mask_kernel(sizes, stride, fork_hbm, owner_hbm, lengths_hbm, *refs):
    *outs, first_ref, fork_ref, owner_ref, lengths_ref, sems = refs
    pairs = ((fork_hbm, fork_ref), (owner_hbm, owner_ref), (lengths_hbm, lengths_ref))
    copies = [pltpu.make_async_copy(src, dst, sems.at[k]) for k, (src, dst) in enumerate(pairs)]
    for copy in copies:
        copy.start()
    for copy in copies:
        copy.wait()
    first_ref[0] = fork_ref[lax.axis_index("ctx")] * stride
    start = 0
    for down_ref, across_ref in zip(outs[::2], outs[1::2], strict=True):
        key = lax.broadcasted_iota(jnp.int32, down_ref.shape, 0) + start
        down_ref[...] = valid_keys(key, *sizes, fork_ref, owner_ref, lengths_ref).astype(F32)
        key = lax.broadcasted_iota(jnp.int32, (8, across_ref.shape[1]), 1) + start
        row = valid_keys(key, *sizes, fork_ref, owner_ref, lengths_ref).astype(F32)
        across_ref[...] = jnp.concatenate([row, row], axis=0).astype(BF16)
        start += down_ref.shape[0]


def split_keys(keys):
    keys = keys * (LOG2E * HD**-0.5)
    high = keys.astype(BF16)
    return jnp.concatenate([high, (keys - high.astype(F32)).astype(BF16)], axis=1)


def shard_keys(shards, seg_rows, prompt_rows, first, mask, fill, g):
    def rows(start, size):
        parts = [r[:, pl.ds(start, size), g * HD : (g + 1) * HD].astype(F32).reshape(-1, HD) for r in shards]
        return jnp.concatenate(parts, axis=0)

    prompt = rows(shards[0].shape[1] - 2 * prompt_rows, 2 * prompt_rows)
    keys = jnp.concatenate([rows(pl.multiple_of(first, 8), seg_rows), prompt], axis=0)
    shifted = pltpu.roll(prompt, prompt.shape[0] - prompt_rows, 0)
    values = jnp.concatenate([rows(pl.multiple_of(first + seg_rows, 8), seg_rows), shifted], axis=0)
    keys = split_keys(jnp.where(mask > 0, keys, fill))
    return keys, jnp.where(mask > 0, values, 0.0).astype(BF16)


def attend(q_ref, ready, causal, take, group):
    span, columns = q_ref.shape[1:]
    kept = {}

    def score(c):
        g = c * PAIR // group
        if g not in kept:
            kept.clear()
            kept[g] = ready(g)
        keys, values = kept[g]
        query = jnp.concatenate([q_ref[0, :, i * HD : (i + 1) * HD] for i in range(c * PAIR, (c + 1) * PAIR)], axis=0)
        query = jnp.concatenate([query, query], axis=1)
        scores = lax.dot_general(keys, query, (((1,), (1,)), ((), ())), preferred_element_type=F32)
        if causal is not None:
            own = scores[:span] + causal
            scores = jnp.concatenate([own, scores[span:]], axis=0) if scores.shape[0] > span else own
        return scores, jnp.max(scores, axis=0, keepdims=True), values

    chunks = columns // HD // PAIR
    made = score(0)
    for c in range(chunks):
        (scores, highest, values), made = made, score(c + 1) if c + 1 < chunks else None

        def weigh(top, scores=scores, values=values):
            weights = jnp.exp2(scores - top).astype(BF16)
            return jnp.dot(values, weights, preferred_element_type=F32)

        take(c, pl.ds(c * PAIR * span, PAIR * span), highest, weigh)


def near_kernel(seg_rows, prompt_rows, first_ref, q_hbm, own_hbm, down_ref, across_ref, *refs):
    *shards, q_ref, state_ref, fill_ref, own_ref, sems = refs
    span = q_ref.shape[1]
    kv_heads = own_ref.shape[2] // HD
    group = q_ref.shape[2] // HD // kv_heads
    own_copy = pltpu.make_async_copy(own_hbm, own_ref, sems.at[kv_heads])
    own_copy.start()
    parts = [pl.ds(g * group * HD, group * HD) for g in range(kv_heads)]
    copies = [pltpu.make_async_copy(q_hbm.at[:, :, p], q_ref.at[:, :, p], sems.at[g]) for g, p in enumerate(parts)]
    for copy in copies:
        copy.start()
    own_copy.wait()
    first = first_ref[0]
    own = jnp.swapaxes(own_ref[...], 0, 1)
    time = lax.broadcasted_iota(jnp.int32, (span, PAIR * span), 1) % span
    causal = jnp.where(lax.broadcasted_iota(jnp.int32, time.shape, 0) <= time, 0.0, -jnp.inf)

    def ready(g):
        copies[g].wait()
        part = slice(g * HD, (g + 1) * HD)
        keys = own[0, :, part].astype(F32)
        fill = keys[0:1]
        fill_ref[g] = jnp.broadcast_to(fill, (8, HD))
        keys, values = split_keys(keys), own[1, :, part]
        if shards:
            more = shard_keys(shards, seg_rows, prompt_rows, first, down_ref[span:], fill, g)
            keys, values = jnp.concatenate([keys, more[0]], axis=0), jnp.concatenate([values, more[1]], axis=0)
        return keys, jnp.concatenate([values.T, across_ref[...]], axis=0)

    def take(c, lanes, highest, weigh):
        state_ref[: HD + 8, lanes] = weigh(highest)[: HD + 8]
        state_ref[HD + 8 :, lanes] = jnp.broadcast_to(highest, (8, highest.shape[1]))

    attend(q_ref, ready, causal, take, group)


def far_kernel(seg_rows, prompt_rows, first_ref, q_ref, state_ref, fill_ref, down_ref, across_ref, *refs):
    *shards, out_ref, stage, sems = refs
    span, columns = q_ref.shape[1:]
    kv_heads = fill_ref.shape[0]
    group = columns // HD // kv_heads
    first = first_ref[0]
    copies = []

    def ready(g):
        keys, values = shard_keys(shards, seg_rows, prompt_rows, first, down_ref[...], fill_ref[g, 0:1], g)
        return keys, jnp.concatenate([values.T, across_ref[...]], axis=0)

    def take(c, lanes, highest, weigh):
        former = state_ref[HD + 8 :, lanes]
        top = jnp.maximum(former, highest)
        both = weigh(top[0:1])
        scale = jnp.exp2(former - top)
        share = 1.0 / (state_ref[HD : HD + 8, lanes] * scale + both[HD : HD + 8])
        scale = scale * share
        rows = (HD // 8, 8, -1)
        result = state_ref[:HD, lanes].reshape(rows) * scale[None] + both[:HD].reshape(rows) * share[None]
        result = result.reshape(HD, -1).astype(BF16)
        for k in range(PAIR):
            i = c * PAIR + k
            stage[:, i * HD : (i + 1) * HD] = result[:, k * span : (k + 1) * span].T
        if (c + 1) * PAIR % group == 0:
            g = c * PAIR // group
            part = pl.ds(g * group * HD, group * HD)
            copies.append(pltpu.make_async_copy(stage.at[:, part], out_ref.at[0, :, part], sems.at[g]))
            copies[-1].start()

    attend(q_ref, ready, None, take, group)
    for copy in copies:
        copy.wait()


def permute(x, target, n):
    return lax.ppermute(x, "ctx", [(i, target(i)) for i in range(n)])


def pair_steps(n):
    return range(n // 4 - 2, 0, -1)


def gather_shards(shard, n):
    far, near = n - 4, 2
    mate = permute(shard, lambda i: i ^ 1, n)
    first = permute(shard, lambda i: i ^ far, n)
    both = jnp.concatenate([shard, mate], axis=0)
    pairs = pair_steps(n)
    wide = [permute(both, lambda i, j=j: i ^ (2 * (2 * j + i % 2)), n) for j in pairs]
    side = permute(shard, lambda i: i ^ near, n)
    passed = permute(first, lambda i: i ^ near, n)
    mine = jnp.concatenate([first, passed, side, *wide], axis=0)
    theirs = permute(mine, lambda i: i ^ 1, n)
    got = [[far, far ^ near, near], [far, far ^ near, near]]
    for j in pairs:
        for core in range(2):
            d = 2 * (2 * j + core)
            got[core] += [d, d ^ 1]
    offsets = [[0, 1, *got[core], *[o ^ 1 for o in got[1 - core]]] for core in range(2)]
    return [shard, mate, mine, theirs], offsets


def use_gather(mesh_size, parents, seg_rows, prompt_rows):
    power = mesh_size >= 8 and mesh_size & (mesh_size - 1) == 0
    return power and parents * seg_rows + prompt_rows <= 2 * (seg_rows + prompt_rows)


def body(child_q, child_kv, prompt_kv, parent_kv, fork_list, owner_map, lengths):
    n = lax.axis_size("ctx")
    seg_rows, prompt_rows = parent_kv.shape[0], prompt_kv.shape[0]
    parents = parent_kv.shape[1]
    span, width = child_kv.shape[1], child_kv.shape[3]
    kv_heads = width // HD
    gather = use_gather(n, parents, seg_rows, prompt_rows)
    if gather:
        rows = 2 * (parents * seg_rows + prompt_rows)
        shard = pl.pallas_call(
            shard_kernel,
            out_shape=jax.ShapeDtypeStruct((rows, width), BF16),
            in_specs=[HBM, HBM],
            out_specs=VMEM,
            scratch_shapes=[
                pltpu.VMEM(prompt_kv.shape, BF16),
                pltpu.VMEM(parent_kv.shape, BF16),
                pltpu.SemaphoreType.DMA((2,)),
            ],
            compiler_params=limit(2),
            name="shard",
        )(*in_hbm(prompt_kv, parent_kv))
        shards, offsets = gather_shards(shard, n)
    else:
        rows = 2 * (seg_rows + prompt_rows)
        send = pl.pallas_call(
            pack_kernel,
            out_shape=jax.ShapeDtypeStruct((n, rows, width), BF16),
            in_specs=[SMEM, VMEM, VMEM],
            out_specs=VMEM,
            scratch_shapes=[pltpu.VMEM((parents, rows, width), BF16)],
            name="pack",
        )(fork_list, prompt_kv, parent_kv)
        shards, offsets = [lax.all_to_all(send, "ctx", split_axis=0, concat_axis=0, tiled=True)], None
    shards = [s.reshape(-1, rows, width) for s in shards]
    near, far = shards[: 2 * gather], shards[2 * gather :]
    counts = [sum(s.shape[0] for s in batch) for batch in (near, far)]
    slots = seg_rows + 2 * prompt_rows
    sizes = [span + counts[0] * slots, counts[1] * slots]
    masks = [jax.ShapeDtypeStruct(*shape) for k in sizes for shape in (((k, HD), F32), ((16, k), BF16))]
    stride = 2 * seg_rows if gather else 0
    near_down, near_across, far_down, far_across, first = pl.pallas_call(
        functools.partial(mask_kernel, (span, seg_rows, prompt_rows, counts, offsets), stride),
        out_shape=[*masks, jax.ShapeDtypeStruct((1,), jnp.int32)],
        in_specs=[HBM] * 3,
        out_specs=[VMEM] * 4 + [SMEM],
        scratch_shapes=[pltpu.SMEM(x.shape, jnp.int32) for x in (fork_list, owner_map, lengths)]
        + [pltpu.SemaphoreType.DMA((3,))],
        compiler_params=limit(4),
        name="mask",
    )(*in_hbm(fork_list, owner_map, lengths))
    query, state, fill = pl.pallas_call(
        functools.partial(near_kernel, seg_rows, prompt_rows),
        out_shape=[
            jax.ShapeDtypeStruct(child_q.shape, BF16),
            jax.ShapeDtypeStruct((HD + 16, child_q.shape[2] // HD * span), F32),
            jax.ShapeDtypeStruct((kv_heads, 8, HD), F32),
        ],
        in_specs=[SMEM, HBM, HBM, VMEM, VMEM] + [VMEM] * len(near),
        out_specs=[VMEM, VMEM, VMEM],
        scratch_shapes=[pltpu.VMEM(child_kv.shape[1:], BF16), pltpu.SemaphoreType.DMA((kv_heads + 1,))],
        compiler_params=limit(16),
        name="near",
    )(first, *in_hbm(child_q, child_kv[0]), near_down, near_across, *near)
    return pl.pallas_call(
        functools.partial(far_kernel, seg_rows, prompt_rows),
        out_shape=jax.ShapeDtypeStruct(child_q.shape, BF16),
        in_specs=[SMEM] + [VMEM] * (5 + len(far)),
        out_specs=HBM,
        scratch_shapes=[pltpu.VMEM(child_q.shape[1:], BF16), pltpu.SemaphoreType.DMA((kv_heads,))],
        compiler_params=limit(16 if gather else 48),
        name="far",
    )(first, query, state, fill, far_down, far_across, *far)


def solution(mesh):
    placed = (
        P(("groups", "ctx"), None, None),
        P(("groups", "ctx"), None, None, None),
        P(("groups", "ctx"), None, None),
        P(("groups", "ctx"), None, None, None),
        P("groups"),
        P("groups", None),
        P("groups"),
    )
    return jax.shard_map(
        body,
        mesh=mesh,
        in_specs=placed,
        out_specs=P(("groups", "ctx"), None, None),
        check_vma=False,
    )
```

```python
import functools

import jax
import jax.numpy as jnp
from jax import lax
from jax.experimental import pallas as pl
from jax.experimental.pallas import tpu as pltpu
from jax.sharding import PartitionSpec as P

HD = 128
LOG2E = 1.4426950408889634
F32 = jnp.float32
BF16 = jnp.bfloat16
NEAR_HEADS, FAR_HEADS = 4, 8
VMEM = pl.BlockSpec(memory_space=pltpu.VMEM)
SMEM = pl.BlockSpec(memory_space=pltpu.SMEM)
HBM = pl.BlockSpec(memory_space=pltpu.HBM)


def in_hbm(*arrays):
    return [pltpu.with_memory_space_constraint(x, pltpu.HBM) for x in arrays]


def limit(mib):
    return pltpu.CompilerParams(vmem_limit_bytes=mib << 20)


def shard_rows(prompt_ref, parent_ref):
    prompt = prompt_ref[...].astype(F32)
    rows = []
    for p in range(parent_ref.shape[1]):
        piece = parent_ref[:, p].astype(F32)
        rows += [piece[:, 0, :], piece[:, 1, :]]
    return rows, [prompt[:, 0, :], prompt[:, 1, :]]


def shard_kernel(prompt_hbm, parent_hbm, out_ref, wide_ref, prompt_ref, parent_ref, sems):
    copies = [
        pltpu.make_async_copy(parent_hbm, parent_ref, sems.at[0]),
        pltpu.make_async_copy(prompt_hbm, prompt_ref, sems.at[1]),
    ]
    for copy in copies:
        copy.start()
    for copy in copies:
        copy.wait()
    pieces, shared = shard_rows(prompt_ref, parent_ref)
    rows = jnp.concatenate(pieces + shared, axis=0)
    out_ref[...] = rows.astype(BF16)
    wide_ref[...] = jnp.concatenate([rows, jnp.zeros_like(rows)], axis=0).astype(BF16)


def pack_kernel(fork_ref, prompt_ref, parent_ref, send_ref, table_ref):
    pieces, shared = shard_rows(prompt_ref, parent_ref)
    for p in range(parent_ref.shape[1]):
        table_ref[p] = jnp.concatenate(pieces[2 * p : 2 * p + 2] + shared, axis=0).astype(BF16)

    def place(d, carry):
        send_ref[d] = table_ref[fork_ref[d]]
        return carry

    lax.fori_loop(0, send_ref.shape[0], place, 0, unroll=min(8, send_ref.shape[0]))


def valid_keys(key, seg_rows, prompt_rows, counts, offsets, fork_ref, owner_ref, lengths_ref):
    n = owner_ref.shape[1]
    device = lax.axis_index("ctx")
    parent = fork_ref[device]
    place, row = jnp.full_like(key, -1), jnp.zeros_like(key)
    prompt = key < 0
    start, shard = 0, 0
    for count in counts:
        slot = key - start
        here = (slot >= 0) & (slot < count * seg_rows)
        place = jnp.where(here, shard + slot // seg_rows, place)
        row = jnp.where(here, slot % seg_rows, row)
        slot = slot - count * seg_rows
        here = (slot >= 0) & (slot < count * 2 * prompt_rows)
        prompt = prompt | (here & (slot % (2 * prompt_rows) < prompt_rows))
        start += count * (seg_rows + 2 * prompt_rows)
        shard += count
    block = place
    if offsets is not None:
        block = jnp.full_like(key, -1)
        for k in range(n):
            owner = device ^ jnp.where(device % 2 == 0, offsets[0][k], offsets[1][k])
            block = jnp.where(place == k, owner, block)

    def step(j, position):
        return jnp.where(block == owner_ref[parent, j], j * seg_rows + row, position)

    beyond = jnp.full_like(key, n * seg_rows)
    position = lax.fori_loop(0, n, step, beyond, unroll=min(16, n))
    return prompt | (position < lengths_ref[parent])


def split_keys(keys):
    keys = keys * (LOG2E * HD**-0.5)
    high = keys.astype(BF16)
    return jnp.concatenate([high, (keys - high.astype(F32)).astype(BF16)], axis=1)


def shard_keys(shards, seg_rows, prompt_rows, first, mask, fill, g):
    def rows(start, size):
        parts = [r[:, pl.ds(start, size), g * HD : (g + 1) * HD].astype(F32).reshape(-1, HD) for r in shards]
        return jnp.concatenate(parts, axis=0)

    prompt = rows(shards[0].shape[1] - 2 * prompt_rows, 2 * prompt_rows)
    keys = jnp.concatenate([rows(pl.multiple_of(first, 8), seg_rows), prompt], axis=0)
    shifted = pltpu.roll(prompt, prompt.shape[0] - prompt_rows, 0)
    values = jnp.concatenate([rows(pl.multiple_of(first + seg_rows, 8), seg_rows), shifted], axis=0)
    keys = split_keys(jnp.where(mask > 0, keys, fill))
    return keys, jnp.where(mask > 0, values, 0.0).astype(BF16)


def attend(q_ref, ready, causal, take, group, many):
    span, columns = q_ref.shape[1:]
    kept = {}

    def score(c):
        g = c * many // group
        if g not in kept:
            kept.clear()
            kept[g] = ready(g)
        keys, values = kept[g]
        query = jnp.concatenate([q_ref[0, :, i * HD : (i + 1) * HD] for i in range(c * many, (c + 1) * many)], axis=0)
        query = jnp.concatenate([query, query], axis=1)
        scores = lax.dot_general(keys, query, (((1,), (1,)), ((), ())), preferred_element_type=F32)
        if causal is not None:
            own = scores[:span] + causal
            scores = jnp.concatenate([own, scores[span:]], axis=0) if scores.shape[0] > span else own
        return scores, jnp.max(scores, axis=0, keepdims=True), values

    chunks = columns // HD // many
    made = score(0)
    for c in range(chunks):
        (scores, highest, values), made = made, score(c + 1) if c + 1 < chunks else None

        def weigh(top, scores=scores, values=values):
            weights = jnp.exp2(scores - top).astype(BF16)
            return jnp.dot(values, weights, preferred_element_type=F32)

        take(c, pl.ds(c * many * span, many * span), highest, weigh)


def near_kernel(sizes, stride, *refs):
    ins, refs = refs[:5], refs[5:]
    q_ref, state_ref, fill_ref, down_ref, across_ref, first_ref, own_ref, own_kv_ref, *tables, sems = refs
    fork_ref, owner_ref, lengths_ref = tables
    span = q_ref.shape[1]
    kv_heads = own_ref.shape[2] // HD
    group = q_ref.shape[2] // HD // kv_heads
    pairs = list(zip(ins[1:], (own_ref, *tables), strict=True))
    for g in range(kv_heads):
        part = pl.ds(g * group * HD, group * HD)
        pairs.append((ins[0].at[:, :, part], q_ref.at[:, :, part]))
    copies = [pltpu.make_async_copy(src, dst, sems.at[k]) for k, (src, dst) in enumerate(pairs)]
    for copy in copies:
        copy.start()
    for copy in copies[:4]:
        copy.wait()
    first_ref[0] = fork_ref[lax.axis_index("ctx")] * stride
    key = lax.broadcasted_iota(jnp.int32, (8, across_ref.shape[1]), 1)
    valid = valid_keys(key, *sizes, fork_ref, owner_ref, lengths_ref).astype(F32)
    across_ref[...] = jnp.concatenate([valid, valid], axis=0).astype(BF16)
    down_ref[...] = jnp.concatenate([valid] * (HD // 8), axis=0).T
    own_kv_ref[...] = jnp.swapaxes(own_ref[...], 0, 1)
    time = lax.broadcasted_iota(jnp.int32, (span, NEAR_HEADS * span), 1) % span
    causal = jnp.where(lax.broadcasted_iota(jnp.int32, time.shape, 0) <= time, 0.0, -jnp.inf)
    ones = jnp.ones((16, span), BF16)

    def ready(g):
        copies[4 + g].wait()
        part = slice(g * HD, (g + 1) * HD)
        keys = own_kv_ref[0, :, part].astype(F32)
        fill_ref[g] = jnp.broadcast_to(keys[0:1], (8, HD))
        return split_keys(keys), jnp.concatenate([own_kv_ref[1, :, part].T, ones], axis=0)

    def take(c, lanes, highest, weigh):
        state_ref[: HD + 8, lanes] = weigh(highest)[: HD + 8]
        state_ref[HD + 8 :, lanes] = jnp.broadcast_to(highest, (8, highest.shape[1]))

    attend(q_ref, ready, causal, take, group, NEAR_HEADS)


def ready_kernel(seg_rows, prompt_rows, first_ref, fill_ref, down_ref, *refs):
    *shards, keys_ref, values_ref = refs
    for g in range(fill_ref.shape[0]):
        mask = down_ref[: keys_ref.shape[1]]
        made = shard_keys(shards, seg_rows, prompt_rows, first_ref[0], mask, fill_ref[g, 0:1], g)
        keys_ref[g], values_ref[g] = made


def far_kernel(seg_rows, prompt_rows, count, first_ref, q_ref, state_ref, fill_ref, down_ref, across_ref, *refs):
    shards, (*former_refs, out_ref, stage, sems) = refs[:count], refs[count:]
    span, columns = q_ref.shape[1:]
    kv_heads = fill_ref.shape[0]
    group = columns // HD // kv_heads
    first = first_ref[0]
    copies = []

    def ready(g):
        known = former_refs[0].shape[1] if former_refs else 0
        keys, values = shard_keys(shards, seg_rows, prompt_rows, first, down_ref[known:], fill_ref[g, 0:1], g)
        if former_refs:
            keys = jnp.concatenate([former_refs[0][g], keys], axis=0)
            values = jnp.concatenate([former_refs[1][g], values], axis=0)
        return keys, jnp.concatenate([values.T, across_ref[...]], axis=0)

    def take(c, lanes, highest, weigh):
        former = state_ref[HD + 8 :, lanes]
        top = jnp.maximum(former, highest)
        both = weigh(top[0:1])
        scale = jnp.exp2(former - top)
        share = 1.0 / (state_ref[HD : HD + 8, lanes] * scale + both[HD : HD + 8])
        scale = scale * share
        rows = (HD // 8, 8, -1)
        result = state_ref[:HD, lanes].reshape(rows) * scale[None] + both[:HD].reshape(rows) * share[None]
        result = result.reshape(HD, -1).astype(BF16)
        for k in range(FAR_HEADS):
            i = c * FAR_HEADS + k
            stage[:, i * HD : (i + 1) * HD] = result[:, k * span : (k + 1) * span].T
        if (c + 1) * FAR_HEADS % group == 0:
            g = c * FAR_HEADS // group
            part = pl.ds(g * group * HD, group * HD)
            copies.append(pltpu.make_async_copy(stage.at[:, part], out_ref.at[0, :, part], sems.at[g]))
            copies[-1].start()

    attend(q_ref, ready, None, take, group, FAR_HEADS)
    for copy in copies:
        copy.wait()


def permute(x, target, n):
    return lax.ppermute(x, "ctx", [(i, target(i)) for i in range(n)])


def pair_steps(n):
    return range(n // 4 - 2, 0, -1)


def gather_shards(shard, both, n):
    far, near = n - 4, 2
    mate = permute(shard, lambda i: i ^ 1, n)
    first = permute(shard, lambda i: i ^ far, n)
    both = lax.dynamic_update_slice(both, mate, (shard.shape[0], 0))
    pairs = pair_steps(n)
    wide = [permute(both, lambda i, j=j: i ^ (2 * (2 * j + i % 2)), n) for j in pairs]
    passed = permute(jnp.concatenate([shard, first], axis=0), lambda i: i ^ near, n)
    mine = jnp.concatenate([first, passed, *wide], axis=0)
    theirs = permute(mine, lambda i: i ^ 1, n)
    got = [[far, near, far ^ near], [far, near, far ^ near]]
    for j in pairs:
        for core in range(2):
            d = 2 * (2 * j + core)
            got[core] += [d, d ^ 1]
    offsets = [[0, 1, *got[core], *[o ^ 1 for o in got[1 - core]]] for core in range(2)]
    return [shard, mate, mine, theirs], offsets


def use_gather(mesh_size, parents, seg_rows, prompt_rows):
    power = mesh_size >= 8 and mesh_size & (mesh_size - 1) == 0
    return power and parents * seg_rows + prompt_rows <= 2 * (seg_rows + prompt_rows)


def body(child_q, child_kv, prompt_kv, parent_kv, fork_list, owner_map, lengths):
    n = lax.axis_size("ctx")
    seg_rows, prompt_rows = parent_kv.shape[0], prompt_kv.shape[0]
    parents = parent_kv.shape[1]
    span, width = child_kv.shape[1], child_kv.shape[3]
    kv_heads = width // HD
    gather = use_gather(n, parents, seg_rows, prompt_rows)
    if gather:
        rows = 2 * (parents * seg_rows + prompt_rows)
        shard, both = pl.pallas_call(
            shard_kernel,
            out_shape=[jax.ShapeDtypeStruct((k * rows, width), BF16) for k in (1, 2)],
            in_specs=[HBM, HBM],
            out_specs=[VMEM, VMEM],
            scratch_shapes=[
                pltpu.VMEM(prompt_kv.shape, BF16),
                pltpu.VMEM(parent_kv.shape, BF16),
                pltpu.SemaphoreType.DMA((2,)),
            ],
            compiler_params=limit(2),
            name="shard",
        )(*in_hbm(prompt_kv, parent_kv))
        shards, offsets = gather_shards(shard, both, n)
    else:
        rows = 2 * (seg_rows + prompt_rows)
        send = pl.pallas_call(
            pack_kernel,
            out_shape=jax.ShapeDtypeStruct((n, rows, width), BF16),
            in_specs=[SMEM, VMEM, VMEM],
            out_specs=VMEM,
            scratch_shapes=[pltpu.VMEM((parents, rows, width), BF16)],
            name="pack",
        )(fork_list, prompt_kv, parent_kv)
        shards, offsets = [lax.all_to_all(send, "ctx", split_axis=0, concat_axis=0, tiled=True)], None
    shards = [s.reshape(-1, rows, width) for s in shards]
    batches = [shards[:-1], shards[-1:]] if gather else [shards]
    counts = [sum(s.shape[0] for s in batch) for batch in batches]
    slots = seg_rows + 2 * prompt_rows
    query, state, fill, down, across, first = pl.pallas_call(
        functools.partial(near_kernel, (seg_rows, prompt_rows, counts, offsets), 2 * seg_rows if gather else 0),
        out_shape=[
            jax.ShapeDtypeStruct(child_q.shape, BF16),
            jax.ShapeDtypeStruct((HD + 16, child_q.shape[2] // HD * span), F32),
            jax.ShapeDtypeStruct((kv_heads, 8, HD), F32),
            jax.ShapeDtypeStruct((n * slots, HD), F32),
            jax.ShapeDtypeStruct((16, n * slots), BF16),
            jax.ShapeDtypeStruct((1,), jnp.int32),
        ],
        in_specs=[HBM] * 5,
        out_specs=[VMEM] * 5 + [SMEM],
        scratch_shapes=[
            pltpu.VMEM(child_kv.shape[1:], BF16),
            pltpu.VMEM((2, span, width), BF16),
            *[pltpu.SMEM(x.shape, jnp.int32) for x in (fork_list, owner_map, lengths)],
            pltpu.SemaphoreType.DMA((4 + kv_heads,)),
        ],
        compiler_params=limit(16),
        name="near",
    )(*in_hbm(child_q, child_kv[0], fork_list, owner_map, lengths))
    former = []
    if gather:
        former = pl.pallas_call(
            functools.partial(ready_kernel, seg_rows, prompt_rows),
            out_shape=[jax.ShapeDtypeStruct((kv_heads, counts[0] * slots, k * HD), BF16) for k in (2, 1)],
            in_specs=[SMEM] + [VMEM] * (2 + len(batches[0])),
            out_specs=[VMEM] * 2,
            compiler_params=limit(4),
            name="ready",
        )(first, fill, down, *batches[0])
    last = batches[-1]
    return pl.pallas_call(
        functools.partial(far_kernel, seg_rows, prompt_rows, len(last)),
        out_shape=jax.ShapeDtypeStruct(child_q.shape, BF16),
        in_specs=[SMEM] + [VMEM] * (5 + len(last) + len(former)),
        out_specs=HBM,
        scratch_shapes=[pltpu.VMEM(child_q.shape[1:], BF16), pltpu.SemaphoreType.DMA((kv_heads,))],
        compiler_params=limit(16 if gather else 48),
        name="far",
    )(first, query, state, fill, down, across, *last, *former)


def solution(mesh):
    placed = (
        P(("groups", "ctx"), None, None),
        P(("groups", "ctx"), None, None, None),
        P(("groups", "ctx"), None, None),
        P(("groups", "ctx"), None, None, None),
        P("groups"),
        P("groups", None),
        P("groups"),
    )
    return jax.shard_map(
        body,
        mesh=mesh,
        in_specs=placed,
        out_specs=P(("groups", "ctx"), None, None),
        check_vma=False,
    )
```

```python
import functools

import jax
import jax.numpy as jnp
from jax import lax
from jax.experimental import pallas as pl
from jax.experimental.pallas import tpu as pltpu
from jax.sharding import PartitionSpec as P

HD = 128
LOG2E = 1.4426950408889634
F32 = jnp.float32
BF16 = jnp.bfloat16
NEAR_HEADS, FAR_HEADS = 4, 8
VMEM = pl.BlockSpec(memory_space=pltpu.VMEM)
SMEM = pl.BlockSpec(memory_space=pltpu.SMEM)
HBM = pl.BlockSpec(memory_space=pltpu.HBM)


def in_hbm(*arrays):
    return [pltpu.with_memory_space_constraint(x, pltpu.HBM) for x in arrays]


def limit(mib):
    return pltpu.CompilerParams(vmem_limit_bytes=mib << 20)


def shard_rows(prompt_ref, parent_ref):
    prompt = prompt_ref[...].astype(F32)
    rows = []
    for p in range(parent_ref.shape[1]):
        piece = parent_ref[:, p].astype(F32)
        rows += [piece[:, 0, :], piece[:, 1, :]]
    return rows, [prompt[:, 0, :], prompt[:, 1, :]]


def shard_kernel(prompt_hbm, parent_hbm, out_ref, wide_ref, prompt_ref, parent_ref, sems):
    copies = [
        pltpu.make_async_copy(parent_hbm, parent_ref, sems.at[0]),
        pltpu.make_async_copy(prompt_hbm, prompt_ref, sems.at[1]),
    ]
    for copy in copies:
        copy.start()
    for copy in copies:
        copy.wait()
    pieces, shared = shard_rows(prompt_ref, parent_ref)
    rows = jnp.concatenate(pieces + shared, axis=0)
    out_ref[...] = rows.astype(BF16)
    wide_ref[...] = jnp.concatenate([rows, jnp.zeros_like(rows)], axis=0).astype(BF16)


def pack_kernel(fork_ref, prompt_ref, parent_ref, send_ref, table_ref):
    pieces, shared = shard_rows(prompt_ref, parent_ref)
    for p in range(parent_ref.shape[1]):
        table_ref[p] = jnp.concatenate(pieces[2 * p : 2 * p + 2] + shared, axis=0).astype(BF16)

    def place(d, carry):
        send_ref[d] = table_ref[fork_ref[d]]
        return carry

    lax.fori_loop(0, send_ref.shape[0], place, 0, unroll=min(8, send_ref.shape[0]))


def valid_keys(key, seg_rows, prompt_rows, counts, offsets, fork_ref, owner_ref, lengths_ref):
    n = owner_ref.shape[1]
    device = lax.axis_index("ctx")
    parent = fork_ref[device]
    place, row = jnp.full_like(key, -1), jnp.zeros_like(key)
    prompt = key < 0
    start, shard = 0, 0
    for count in counts:
        slot = key - start
        here = (slot >= 0) & (slot < count * seg_rows)
        place = jnp.where(here, shard + slot // seg_rows, place)
        row = jnp.where(here, slot % seg_rows, row)
        slot = slot - count * seg_rows
        here = (slot >= 0) & (slot < count * 2 * prompt_rows)
        prompt = prompt | (here & (slot % (2 * prompt_rows) < prompt_rows))
        start += count * (seg_rows + 2 * prompt_rows)
        shard += count
    block = place
    if offsets is not None:
        block = jnp.full_like(key, -1)
        for k in range(n):
            owner = device ^ jnp.where(device % 2 == 0, offsets[0][k], offsets[1][k])
            block = jnp.where(place == k, owner, block)

    def step(j, position):
        return jnp.where(block == owner_ref[parent, j], j * seg_rows + row, position)

    beyond = jnp.full_like(key, n * seg_rows)
    position = lax.fori_loop(0, n, step, beyond, unroll=min(16, n))
    return prompt | (position < lengths_ref[parent])


def split_keys(keys):
    keys = keys * (LOG2E * HD**-0.5)
    high = keys.astype(BF16)
    return jnp.concatenate([high, (keys - high.astype(F32)).astype(BF16)], axis=1)


def shard_keys(shards, seg_rows, prompt_rows, choice_ref, mask, fill, g):
    def rows(start, size):
        parts = [r[:, pl.ds(start, size), g * HD : (g + 1) * HD].astype(F32).reshape(-1, HD) for r in shards]
        return jnp.concatenate(parts, axis=0)

    def parent_rows(start):
        found = rows(start, seg_rows)
        for p in range(1, choice_ref.shape[0]):
            chosen = choice_ref[p, 0:1, :] > 0
            found = jnp.where(chosen, rows(start + p * 2 * seg_rows, seg_rows), found)
        return found

    prompt = rows(shards[0].shape[1] - 2 * prompt_rows, 2 * prompt_rows)
    keys = jnp.concatenate([parent_rows(0), prompt], axis=0)
    shifted = pltpu.roll(prompt, prompt.shape[0] - prompt_rows, 0)
    values = jnp.concatenate([parent_rows(seg_rows), shifted], axis=0)
    keys = split_keys(jnp.where(mask > 0, keys, fill))
    return keys, jnp.where(mask > 0, values, 0.0).astype(BF16)


def attend(q_ref, ready, causal, take, group, many):
    span, columns = q_ref.shape[1:]
    kept = {}

    def score(c):
        g = c * many // group
        if g not in kept:
            kept.clear()
            kept[g] = ready(g)
        keys, values = kept[g]
        query = jnp.concatenate([q_ref[0, :, i * HD : (i + 1) * HD] for i in range(c * many, (c + 1) * many)], axis=0)
        query = jnp.concatenate([query, query], axis=1)
        scores = lax.dot_general(keys, query, (((1,), (1,)), ((), ())), preferred_element_type=F32)
        if causal is not None:
            own = scores[:span] + causal
            scores = jnp.concatenate([own, scores[span:]], axis=0) if scores.shape[0] > span else own
        return scores, jnp.max(scores, axis=0, keepdims=True), values

    chunks = columns // HD // many
    made = score(0)
    for c in range(chunks):
        (scores, highest, values), made = made, score(c + 1) if c + 1 < chunks else None

        def weigh(top, scores=scores, values=values):
            weights = jnp.exp2(scores - top).astype(BF16)
            return jnp.dot(values, weights, preferred_element_type=F32)

        take(c, pl.ds(c * many * span, many * span), highest, weigh)


def near_kernel(sizes, *refs):
    ins, refs = refs[:5], refs[5:]
    q_ref, state_ref, fill_ref, down_ref, across_ref, choice_ref, own_ref, own_kv_ref, *tables, sems = refs
    fork_ref, owner_ref, lengths_ref = tables
    span = q_ref.shape[1]
    kv_heads = own_ref.shape[2] // HD
    group = q_ref.shape[2] // HD // kv_heads
    pairs = list(zip(ins[1:], (own_ref, *tables), strict=True))
    for g in range(kv_heads):
        part = pl.ds(g * group * HD, group * HD)
        pairs.append((ins[0].at[:, :, part], q_ref.at[:, :, part]))
    copies = [pltpu.make_async_copy(src, dst, sems.at[k]) for k, (src, dst) in enumerate(pairs)]
    for copy in copies:
        copy.start()
    for copy in copies[:4]:
        copy.wait()
    parent = fork_ref[lax.axis_index("ctx")]
    for p in range(choice_ref.shape[0]):
        choice_ref[p] = jnp.full((8, HD), jnp.where(parent == p, 1.0, 0.0), F32)
    key = lax.broadcasted_iota(jnp.int32, (8, across_ref.shape[1]), 1)
    valid = valid_keys(key, *sizes, fork_ref, owner_ref, lengths_ref).astype(F32)
    across_ref[...] = jnp.concatenate([valid, valid], axis=0).astype(BF16)
    down_ref[...] = jnp.concatenate([valid] * (HD // 8), axis=0).T
    own_kv_ref[...] = jnp.swapaxes(own_ref[...], 0, 1)
    time = lax.broadcasted_iota(jnp.int32, (span, NEAR_HEADS * span), 1) % span
    causal = jnp.where(lax.broadcasted_iota(jnp.int32, time.shape, 0) <= time, 0.0, -jnp.inf)
    ones = jnp.ones((16, span), BF16)

    def ready(g):
        copies[4 + g].wait()
        part = slice(g * HD, (g + 1) * HD)
        keys = own_kv_ref[0, :, part].astype(F32)
        fill_ref[g] = jnp.broadcast_to(keys[0:1], (8, HD))
        return split_keys(keys), jnp.concatenate([own_kv_ref[1, :, part].T, ones], axis=0)

    def take(c, lanes, highest, weigh):
        state_ref[: HD + 8, lanes] = weigh(highest)[: HD + 8]
        state_ref[HD + 8 :, lanes] = jnp.broadcast_to(highest, (8, highest.shape[1]))

    attend(q_ref, ready, causal, take, group, NEAR_HEADS)


def ready_kernel(seg_rows, prompt_rows, choice_ref, fill_ref, down_ref, *refs):
    *shards, keys_ref, values_ref = refs
    for g in range(fill_ref.shape[0]):
        mask = down_ref[: keys_ref.shape[1]]
        made = shard_keys(shards, seg_rows, prompt_rows, choice_ref, mask, fill_ref[g, 0:1], g)
        keys_ref[g], values_ref[g] = made


def far_kernel(seg_rows, prompt_rows, count, choice_ref, q_ref, state_ref, fill_ref, down_ref, across_ref, *refs):
    shards, (*former_refs, out_ref, stage, sems) = refs[:count], refs[count:]
    span, columns = q_ref.shape[1:]
    kv_heads = fill_ref.shape[0]
    group = columns // HD // kv_heads
    copies = []

    def ready(g):
        known = former_refs[0].shape[1] if former_refs else 0
        keys, values = shard_keys(shards, seg_rows, prompt_rows, choice_ref, down_ref[known:], fill_ref[g, 0:1], g)
        if former_refs:
            keys = jnp.concatenate([former_refs[0][g], keys], axis=0)
            values = jnp.concatenate([former_refs[1][g], values], axis=0)
        return keys, jnp.concatenate([values.T, across_ref[...]], axis=0)

    def take(c, lanes, highest, weigh):
        former = state_ref[HD + 8 :, lanes]
        top = jnp.maximum(former, highest)
        both = weigh(top[0:1])
        scale = jnp.exp2(former - top)
        share = 1.0 / (state_ref[HD : HD + 8, lanes] * scale + both[HD : HD + 8])
        scale = scale * share
        rows = (HD // 8, 8, -1)
        result = state_ref[:HD, lanes].reshape(rows) * scale[None] + both[:HD].reshape(rows) * share[None]
        result = result.reshape(HD, -1).astype(BF16)
        for k in range(FAR_HEADS):
            i = c * FAR_HEADS + k
            stage[:, i * HD : (i + 1) * HD] = result[:, k * span : (k + 1) * span].T
        if (c + 1) * FAR_HEADS % group == 0:
            g = c * FAR_HEADS // group
            part = pl.ds(g * group * HD, group * HD)
            copies.append(pltpu.make_async_copy(stage.at[:, part], out_ref.at[0, :, part], sems.at[g]))
            copies[-1].start()

    attend(q_ref, ready, None, take, group, FAR_HEADS)
    for copy in copies:
        copy.wait()


def permute(x, target, n):
    return lax.ppermute(x, "ctx", [(i, target(i)) for i in range(n)])


def pair_steps(n):
    return range(n // 4 - 2, 0, -1)


def gather_shards(shard, both, n):
    far, near = n - 4, 2
    mate = permute(shard, lambda i: i ^ 1, n)
    first = permute(shard, lambda i: i ^ far, n)
    both = lax.dynamic_update_slice(both, mate, (shard.shape[0], 0))
    pairs = pair_steps(n)
    wide = [permute(both, lambda i, j=j: i ^ (2 * (2 * j + i % 2)), n) for j in pairs]
    side = permute(shard, lambda i: i ^ near, n)
    passed = permute(first, lambda i: i ^ near, n)
    mine = jnp.concatenate([first, *wide, side, passed], axis=0)
    theirs = permute(mine, lambda i: i ^ 1, n)
    got = []
    for core in range(2):
        steps = [2 * (2 * j + core) for j in pairs]
        got.append([far, *[o for d in steps for o in (d, d ^ 1)], near, far ^ near])
    offsets = [[0, 1, *got[core], *[o ^ 1 for o in got[1 - core]]] for core in range(2)]
    return [shard, mate, mine, theirs], offsets


def use_gather(mesh_size, parents, seg_rows, prompt_rows):
    power = mesh_size >= 8 and mesh_size & (mesh_size - 1) == 0
    return power and parents * seg_rows + prompt_rows <= 2 * (seg_rows + prompt_rows)


def body(child_q, child_kv, prompt_kv, parent_kv, fork_list, owner_map, lengths):
    n = lax.axis_size("ctx")
    seg_rows, prompt_rows = parent_kv.shape[0], prompt_kv.shape[0]
    parents = parent_kv.shape[1]
    span, width = child_kv.shape[1], child_kv.shape[3]
    kv_heads = width // HD
    gather = use_gather(n, parents, seg_rows, prompt_rows)
    if gather:
        rows = 2 * (parents * seg_rows + prompt_rows)
        shard, both = pl.pallas_call(
            shard_kernel,
            out_shape=[jax.ShapeDtypeStruct((k * rows, width), BF16) for k in (1, 2)],
            in_specs=[HBM, HBM],
            out_specs=[VMEM, VMEM],
            scratch_shapes=[
                pltpu.VMEM(prompt_kv.shape, BF16),
                pltpu.VMEM(parent_kv.shape, BF16),
                pltpu.SemaphoreType.DMA((2,)),
            ],
            compiler_params=limit(2),
            name="shard",
        )(*in_hbm(prompt_kv, parent_kv))
        shards, offsets = gather_shards(shard, both, n)
    else:
        rows = 2 * (seg_rows + prompt_rows)
        send = pl.pallas_call(
            pack_kernel,
            out_shape=jax.ShapeDtypeStruct((n, rows, width), BF16),
            in_specs=[SMEM, VMEM, VMEM],
            out_specs=VMEM,
            scratch_shapes=[pltpu.VMEM((parents, rows, width), BF16)],
            name="pack",
        )(fork_list, prompt_kv, parent_kv)
        shards, offsets = [lax.all_to_all(send, "ctx", split_axis=0, concat_axis=0, tiled=True)], None
    shards = [s.reshape(-1, rows, width) for s in shards]
    batches = [shards[:-1], shards[-1:]] if gather else [shards]
    counts = [sum(s.shape[0] for s in batch) for batch in batches]
    slots = seg_rows + 2 * prompt_rows
    query, state, fill, down, across, choice = pl.pallas_call(
        functools.partial(near_kernel, (seg_rows, prompt_rows, counts, offsets)),
        out_shape=[
            jax.ShapeDtypeStruct(child_q.shape, BF16),
            jax.ShapeDtypeStruct((HD + 16, child_q.shape[2] // HD * span), F32),
            jax.ShapeDtypeStruct((kv_heads, 8, HD), F32),
            jax.ShapeDtypeStruct((n * slots, HD), F32),
            jax.ShapeDtypeStruct((16, n * slots), BF16),
            jax.ShapeDtypeStruct((parents if gather else 1, 8, HD), F32),
        ],
        in_specs=[HBM] * 5,
        out_specs=[VMEM] * 6,
        scratch_shapes=[
            pltpu.VMEM(child_kv.shape[1:], BF16),
            pltpu.VMEM((2, span, width), BF16),
            *[pltpu.SMEM(x.shape, jnp.int32) for x in (fork_list, owner_map, lengths)],
            pltpu.SemaphoreType.DMA((4 + kv_heads,)),
        ],
        compiler_params=limit(16),
        name="near",
    )(*in_hbm(child_q, child_kv[0], fork_list, owner_map, lengths))
    former = []
    if gather:
        former = pl.pallas_call(
            functools.partial(ready_kernel, seg_rows, prompt_rows),
            out_shape=[jax.ShapeDtypeStruct((kv_heads, counts[0] * slots, k * HD), BF16) for k in (2, 1)],
            in_specs=[VMEM] * (3 + len(batches[0])),
            out_specs=[VMEM] * 2,
            compiler_params=limit(4),
            name="ready",
        )(choice, fill, down, *batches[0])
    last = batches[-1]
    return pl.pallas_call(
        functools.partial(far_kernel, seg_rows, prompt_rows, len(last)),
        out_shape=jax.ShapeDtypeStruct(child_q.shape, BF16),
        in_specs=[VMEM] * (6 + len(last) + len(former)),
        out_specs=HBM,
        scratch_shapes=[pltpu.VMEM(child_q.shape[1:], BF16), pltpu.SemaphoreType.DMA((kv_heads,))],
        compiler_params=limit(16 if gather else 48),
        name="far",
    )(choice, query, state, fill, down, across, *last, *former)


def solution(mesh):
    placed = (
        P(("groups", "ctx"), None, None),
        P(("groups", "ctx"), None, None, None),
        P(("groups", "ctx"), None, None),
        P(("groups", "ctx"), None, None, None),
        P("groups"),
        P("groups", None),
        P("groups"),
    )
    return jax.shard_map(
        body,
        mesh=mesh,
        in_specs=placed,
        out_specs=P(("groups", "ctx"), None, None),
        check_vma=False,
    )
```

```python
import functools

import jax
import jax.numpy as jnp
from jax import lax
from jax.experimental import pallas as pl
from jax.experimental.pallas import tpu as pltpu
from jax.sharding import PartitionSpec as P

HD = 128
LOG2E = 1.4426950408889634
F32 = jnp.float32
BF16 = jnp.bfloat16
NEAR_HEADS, FAR_HEADS, OUT_HEADS, LOADS = 8, 8, 8, 4
VMEM = pl.BlockSpec(memory_space=pltpu.VMEM)
SMEM = pl.BlockSpec(memory_space=pltpu.SMEM)
HBM = pl.BlockSpec(memory_space=pltpu.HBM)


def in_hbm(*arrays):
    return [pltpu.with_memory_space_constraint(x, pltpu.HBM) for x in arrays]


def limit(mib):
    return pltpu.CompilerParams(vmem_limit_bytes=mib << 20)


def shard_rows(prompt_ref, parent_ref):
    prompt = prompt_ref[...].astype(F32)
    rows = []
    for p in range(parent_ref.shape[1]):
        piece = parent_ref[:, p].astype(F32)
        rows += [piece[:, 0, :], piece[:, 1, :]]
    return rows, [prompt[:, 0, :], prompt[:, 1, :]]


def shard_kernel(prompt_hbm, parent_hbm, out_ref, wide_ref, prompt_ref, parent_ref, sems):
    copies = [
        pltpu.make_async_copy(parent_hbm, parent_ref, sems.at[0]),
        pltpu.make_async_copy(prompt_hbm, prompt_ref, sems.at[1]),
    ]
    for copy in copies:
        copy.start()
    for copy in copies:
        copy.wait()
    pieces, shared = shard_rows(prompt_ref, parent_ref)
    rows = jnp.concatenate(pieces + shared, axis=0)
    out_ref[...] = rows.astype(BF16)
    wide_ref[...] = jnp.concatenate([rows, jnp.zeros_like(rows)], axis=0).astype(BF16)


def pack_kernel(fork_ref, prompt_ref, parent_ref, send_ref, table_ref):
    pieces, shared = shard_rows(prompt_ref, parent_ref)
    for p in range(parent_ref.shape[1]):
        table_ref[p] = jnp.concatenate(pieces[2 * p : 2 * p + 2] + shared, axis=0).astype(BF16)

    def place(d, carry):
        send_ref[d] = table_ref[fork_ref[d]]
        return carry

    lax.fori_loop(0, send_ref.shape[0], place, 0, unroll=min(8, send_ref.shape[0]))


def valid_keys(key, seg_rows, prompt_rows, counts, offsets, fork_ref, owner_ref, lengths_ref):
    n = owner_ref.shape[1]
    device = lax.axis_index("ctx")
    parent = fork_ref[device]
    place, row = jnp.full_like(key, -1), jnp.zeros_like(key)
    prompt = key < 0
    start, shard = 0, 0
    for count in counts:
        slot = key - start
        here = (slot >= 0) & (slot < count * seg_rows)
        place = jnp.where(here, shard + slot // seg_rows, place)
        row = jnp.where(here, slot % seg_rows, row)
        slot = slot - count * seg_rows
        here = (slot >= 0) & (slot < count * 2 * prompt_rows)
        prompt = prompt | (here & (slot % (2 * prompt_rows) < prompt_rows))
        start += count * (seg_rows + 2 * prompt_rows)
        shard += count
    block = place
    if offsets is not None:
        block = jnp.full_like(key, -1)
        for k in range(n):
            owner = device ^ jnp.where(device % 2 == 0, offsets[0][k], offsets[1][k])
            block = jnp.where(place == k, owner, block)

    def step(j, position):
        return jnp.where(block == owner_ref[parent, j], j * seg_rows + row, position)

    beyond = jnp.full_like(key, n * seg_rows)
    position = lax.fori_loop(0, n, step, beyond, unroll=min(16, n))
    return prompt | (position < lengths_ref[parent])


def split_keys(keys):
    keys = keys * (LOG2E * HD**-0.5)
    high = keys.astype(BF16)
    return jnp.concatenate([high, (keys - high.astype(F32)).astype(BF16)], axis=1)


def shard_keys(shards, seg_rows, prompt_rows, choice_ref, mask, fill, g):
    def rows(start, size):
        parts = [r[:, pl.ds(start, size), g * HD : (g + 1) * HD].astype(F32).reshape(-1, HD) for r in shards]
        return jnp.concatenate(parts, axis=0)

    def parent_rows(start):
        found = rows(start, seg_rows)
        for p in range(1, choice_ref.shape[0]):
            chosen = choice_ref[p, 0:1, :] > 0
            found = jnp.where(chosen, rows(start + p * 2 * seg_rows, seg_rows), found)
        return found

    prompt = rows(shards[0].shape[1] - 2 * prompt_rows, 2 * prompt_rows)
    keys = jnp.concatenate([parent_rows(0), prompt], axis=0)
    shifted = pltpu.roll(prompt, prompt.shape[0] - prompt_rows, 0)
    values = jnp.concatenate([parent_rows(seg_rows), shifted], axis=0)
    keys = split_keys(jnp.where(mask > 0, keys, fill))
    return keys, jnp.where(mask > 0, values, 0.0).astype(BF16)


def attend(q_ref, ready, causal, take, group, many):
    span, columns = q_ref.shape[1:]
    kept = {}

    def score(c):
        g = c * many // group
        if g not in kept:
            kept.clear()
            kept[g] = ready(g)
        keys, values = kept[g]
        query = jnp.concatenate([q_ref[0, :, i * HD : (i + 1) * HD] for i in range(c * many, (c + 1) * many)], axis=0)
        query = jnp.concatenate([query, query], axis=1)
        scores = lax.dot_general(keys, query, (((1,), (1,)), ((), ())), preferred_element_type=F32)
        if causal is not None:
            own = scores[:span] + causal
            scores = jnp.concatenate([own, scores[span:]], axis=0) if scores.shape[0] > span else own
        return scores, jnp.max(scores, axis=0, keepdims=True), values

    chunks = columns // HD // many
    made = score(0)
    for c in range(chunks):
        (scores, highest, values), made = made, score(c + 1) if c + 1 < chunks else None

        def weigh(top, scores=scores, values=values):
            weights = jnp.exp2(scores - top).astype(BF16)
            return jnp.dot(values, weights, preferred_element_type=F32)

        take(c, pl.ds(c * many * span, many * span), highest, weigh)


def load_kernel(sizes, *refs):
    ins, (q_ref, own_ref, down_ref, across_ref, choice_ref, raw_ref, *tables, sems) = refs[:5], refs[5:]
    fork_ref, owner_ref, lengths_ref = tables
    pairs = list(zip(ins, (*tables, raw_ref), strict=False))
    rows = q_ref.shape[1] // LOADS
    for k in range(LOADS):
        pairs.append((ins[4].at[:, pl.ds(k * rows, rows)], q_ref.at[:, pl.ds(k * rows, rows)]))
    copies = [pltpu.make_async_copy(src, dst, sems.at[k]) for k, (src, dst) in enumerate(pairs)]
    for copy in copies:
        copy.start()
    for copy in copies[:3]:
        copy.wait()
    parent = fork_ref[lax.axis_index("ctx")]
    for p in range(choice_ref.shape[0]):
        choice_ref[p] = jnp.full((8, HD), jnp.where(parent == p, 1.0, 0.0), F32)
    key = lax.broadcasted_iota(jnp.int32, (8, across_ref.shape[1]), 1)
    valid = valid_keys(key, *sizes, fork_ref, owner_ref, lengths_ref).astype(F32)
    across_ref[...] = jnp.concatenate([valid, valid], axis=0).astype(BF16)
    down_ref[...] = jnp.concatenate([valid] * (HD // 8), axis=0).T
    copies[3].wait()
    own_ref[...] = jnp.swapaxes(raw_ref[...], 0, 1)
    for copy in copies[4:]:
        copy.wait()


def near_kernel(q_ref, own_ref, state_ref, fill_ref):
    span = q_ref.shape[1]
    kv_heads = own_ref.shape[2] // HD
    group = q_ref.shape[2] // HD // kv_heads
    time = lax.broadcasted_iota(jnp.int32, (span, NEAR_HEADS * span), 1) % span
    causal = jnp.where(lax.broadcasted_iota(jnp.int32, time.shape, 0) <= time, 0.0, -jnp.inf)
    ones = jnp.ones((16, span), BF16)

    def ready(g):
        part = slice(g * HD, (g + 1) * HD)
        keys = own_ref[0, :, part].astype(F32)
        fill_ref[g] = jnp.broadcast_to(keys[0:1], (8, HD))
        return split_keys(keys), jnp.concatenate([own_ref[1, :, part].T, ones], axis=0)

    def take(c, lanes, highest, weigh):
        state_ref[: HD + 8, lanes] = weigh(highest)[: HD + 8]
        state_ref[HD + 8 :, lanes] = jnp.broadcast_to(highest, (8, highest.shape[1]))

    attend(q_ref, ready, causal, take, group, NEAR_HEADS)


def ready_kernel(seg_rows, prompt_rows, start, choice_ref, fill_ref, down_ref, *refs):
    *shards, keys_ref, values_ref = refs
    for g in range(fill_ref.shape[0]):
        mask = down_ref[start : start + keys_ref.shape[1]]
        made = shard_keys(shards, seg_rows, prompt_rows, choice_ref, mask, fill_ref[g, 0:1], g)
        keys_ref[g], values_ref[g] = made


def far_kernel(seg_rows, prompt_rows, count, choice_ref, q_ref, state_ref, fill_ref, down_ref, across_ref, *refs):
    shards, (*former_refs, out_ref, stage, sems) = refs[:count], refs[count:]
    span, columns = q_ref.shape[1:]
    kv_heads = fill_ref.shape[0]
    group = columns // HD // kv_heads
    copies = []

    def ready(g):
        known = sum(r.shape[1] for r in former_refs[::2])
        keys, values = shard_keys(shards, seg_rows, prompt_rows, choice_ref, down_ref[known:], fill_ref[g, 0:1], g)
        if former_refs:
            keys = jnp.concatenate([*[r[g] for r in former_refs[::2]], keys], axis=0)
            values = jnp.concatenate([*[r[g] for r in former_refs[1::2]], values], axis=0)
        return keys, jnp.concatenate([values.T, across_ref[...]], axis=0)

    def take(c, lanes, highest, weigh):
        former = state_ref[HD + 8 :, lanes]
        top = jnp.maximum(former, highest)
        both = weigh(top[0:1])
        scale = jnp.exp2(former - top)
        share = 1.0 / (state_ref[HD : HD + 8, lanes] * scale + both[HD : HD + 8])
        scale = scale * share
        rows = (HD // 8, 8, -1)
        result = state_ref[:HD, lanes].reshape(rows) * scale[None] + both[:HD].reshape(rows) * share[None]
        result = result.reshape(HD, -1).astype(BF16)
        for k in range(FAR_HEADS):
            i = c * FAR_HEADS + k
            stage[:, i * HD : (i + 1) * HD] = result[:, k * span : (k + 1) * span].T
            if (i + 1) % OUT_HEADS == 0:
                part = pl.ds((i + 1 - OUT_HEADS) * HD, OUT_HEADS * HD)
                copies.append(pltpu.make_async_copy(stage.at[:, part], out_ref.at[0, :, part], sems.at[len(copies)]))
                copies[-1].start()

    attend(q_ref, ready, None, take, group, FAR_HEADS)
    for copy in copies:
        copy.wait()


def permute(x, target, n):
    return lax.ppermute(x, "ctx", [(i, target(i)) for i in range(n)])


def pair_steps(n):
    return range(n // 4 - 2, 0, -1)


def gather_shards(shard, both, n):
    far, near = n - 4, 2
    mate = permute(shard, lambda i: i ^ 1, n)
    first = permute(shard, lambda i: i ^ far, n)
    both = lax.dynamic_update_slice(both, mate, (shard.shape[0], 0))
    pairs = pair_steps(n)
    wide = [permute(both, lambda i, j=j: i ^ (2 * (2 * j + i % 2)), n) for j in pairs]
    side = permute(shard, lambda i: i ^ near, n)
    passed = permute(first, lambda i: i ^ near, n)
    soon = jnp.concatenate([first, side, *wide[1:]], axis=0)
    late = jnp.concatenate([*wide[:1], passed], axis=0)
    soon_theirs = permute(soon, lambda i: i ^ 1, n)
    late_theirs = permute(late, lambda i: i ^ 1, n)
    got = []
    for core in range(2):
        steps = [[2 * (2 * j + core), 2 * (2 * j + core) ^ 1] for j in pairs]
        got.append(([far, near, *[o for step in steps[1:] for o in step]], [*steps[0], far ^ near]))
    offsets = []
    for core in range(2):
        theirs = [[o ^ 1 for o in part] for part in got[1 - core]]
        offsets.append([0, 1, *got[core][0], *theirs[0], *got[core][1], *theirs[1]])
    return [[shard, mate, soon], [soon_theirs, late], [late_theirs]], offsets


def use_gather(mesh_size, parents, seg_rows, prompt_rows):
    power = mesh_size >= 8 and mesh_size & (mesh_size - 1) == 0
    return power and parents * seg_rows + prompt_rows <= 2 * (seg_rows + prompt_rows)


def body(child_q, child_kv, prompt_kv, parent_kv, fork_list, owner_map, lengths):
    n = lax.axis_size("ctx")
    seg_rows, prompt_rows = parent_kv.shape[0], prompt_kv.shape[0]
    parents = parent_kv.shape[1]
    span, width = child_kv.shape[1], child_kv.shape[3]
    kv_heads = width // HD
    gather = use_gather(n, parents, seg_rows, prompt_rows)
    if gather:
        rows = 2 * (parents * seg_rows + prompt_rows)
        shard, both = pl.pallas_call(
            shard_kernel,
            out_shape=[jax.ShapeDtypeStruct((k * rows, width), BF16) for k in (1, 2)],
            in_specs=[HBM, HBM],
            out_specs=[VMEM, VMEM],
            scratch_shapes=[
                pltpu.VMEM(prompt_kv.shape, BF16),
                pltpu.VMEM(parent_kv.shape, BF16),
                pltpu.SemaphoreType.DMA((2,)),
            ],
            compiler_params=limit(2),
            name="shard",
        )(*in_hbm(prompt_kv, parent_kv))
        batches, offsets = gather_shards(shard, both, n)
    else:
        rows = 2 * (seg_rows + prompt_rows)
        send = pl.pallas_call(
            pack_kernel,
            out_shape=jax.ShapeDtypeStruct((n, rows, width), BF16),
            in_specs=[SMEM, VMEM, VMEM],
            out_specs=VMEM,
            scratch_shapes=[pltpu.VMEM((parents, rows, width), BF16)],
            name="pack",
        )(fork_list, prompt_kv, parent_kv)
        batches, offsets = [[lax.all_to_all(send, "ctx", split_axis=0, concat_axis=0, tiled=True)]], None
    batches = [[s.reshape(-1, rows, width) for s in batch] for batch in batches]
    counts = [sum(s.shape[0] for s in batch) for batch in batches]
    slots = seg_rows + 2 * prompt_rows
    query, own, down, across, choice = pl.pallas_call(
        functools.partial(load_kernel, (seg_rows, prompt_rows, counts, offsets)),
        out_shape=[
            jax.ShapeDtypeStruct(child_q.shape, BF16),
            jax.ShapeDtypeStruct((2, span, width), BF16),
            jax.ShapeDtypeStruct((n * slots, HD), F32),
            jax.ShapeDtypeStruct((16, n * slots), BF16),
            jax.ShapeDtypeStruct((parents if gather else 1, 8, HD), F32),
        ],
        in_specs=[HBM] * 5,
        out_specs=[VMEM] * 5,
        scratch_shapes=[
            pltpu.VMEM(child_kv.shape[1:], BF16),
            *[pltpu.SMEM(x.shape, jnp.int32) for x in (fork_list, owner_map, lengths)],
            pltpu.SemaphoreType.DMA((4 + LOADS,)),
        ],
        compiler_params=limit(8),
        name="load",
    )(*in_hbm(fork_list, owner_map, lengths, child_kv[0], child_q))
    state, fill = pl.pallas_call(
        near_kernel,
        out_shape=[
            jax.ShapeDtypeStruct((HD + 16, child_q.shape[2] // HD * span), F32),
            jax.ShapeDtypeStruct((kv_heads, 8, HD), F32),
        ],
        in_specs=[VMEM] * 2,
        out_specs=[VMEM] * 2,
        compiler_params=limit(16),
        name="near",
    )(query, own)
    former = []
    for k, (batch, count) in enumerate(zip(batches[:-1], counts)):
        former += pl.pallas_call(
            functools.partial(ready_kernel, seg_rows, prompt_rows, sum(counts[:k]) * slots),
            out_shape=[jax.ShapeDtypeStruct((kv_heads, count * slots, k * HD), BF16) for k in (2, 1)],
            in_specs=[VMEM] * (3 + len(batch)),
            out_specs=[VMEM] * 2,
            compiler_params=limit(4),
        )(choice, fill, down, *batch)
    last = batches[-1]
    return pl.pallas_call(
        functools.partial(far_kernel, seg_rows, prompt_rows, len(last)),
        out_shape=jax.ShapeDtypeStruct(child_q.shape, BF16),
        in_specs=[VMEM] * (6 + len(last) + len(former)),
        out_specs=HBM,
        scratch_shapes=[pltpu.VMEM(child_q.shape[1:], BF16), pltpu.SemaphoreType.DMA((child_q.shape[2] // HD // OUT_HEADS,))],
        compiler_params=limit(16 if gather else 48),
        name="far",
    )(choice, query, state, fill, down, across, *last, *former)


def solution(mesh):
    placed = (
        P(("groups", "ctx"), None, None),
        P(("groups", "ctx"), None, None, None),
        P(("groups", "ctx"), None, None),
        P(("groups", "ctx"), None, None, None),
        P("groups"),
        P("groups", None),
        P("groups"),
    )
    return jax.shard_map(
        body,
        mesh=mesh,
        in_specs=placed,
        out_specs=P(("groups", "ctx"), None, None),
        check_vma=False,
    )
```

```python
import functools

import jax
import jax.numpy as jnp
from jax import lax
from jax.experimental import pallas as pl
from jax.experimental.pallas import tpu as pltpu
from jax.sharding import PartitionSpec as P

HD = 128
LOG2E = 1.4426950408889634
F32 = jnp.float32
BF16 = jnp.bfloat16
NEAR_HEADS, JOIN_HEADS, LAST_HEADS, OUT_HEADS, LOADS = 8, 8, 8, 8, 4
VMEM = pl.BlockSpec(memory_space=pltpu.VMEM)
SMEM = pl.BlockSpec(memory_space=pltpu.SMEM)
HBM = pl.BlockSpec(memory_space=pltpu.HBM)


def in_hbm(*arrays):
    return [pltpu.with_memory_space_constraint(x, pltpu.HBM) for x in arrays]


def limit(mib):
    return pltpu.CompilerParams(vmem_limit_bytes=mib << 20)


def shard_rows(prompt_ref, parent_ref):
    prompt = prompt_ref[...].astype(F32)
    rows = []
    for p in range(parent_ref.shape[1]):
        piece = parent_ref[:, p].astype(F32)
        rows += [piece[:, 0, :], piece[:, 1, :]]
    return rows, [prompt[:, 0, :], prompt[:, 1, :]]


def shard_kernel(prompt_hbm, parent_hbm, out_ref, wide_ref, prompt_ref, parent_ref, sems):
    copies = [
        pltpu.make_async_copy(parent_hbm, parent_ref, sems.at[0]),
        pltpu.make_async_copy(prompt_hbm, prompt_ref, sems.at[1]),
    ]
    for copy in copies:
        copy.start()
    for copy in copies:
        copy.wait()
    pieces, shared = shard_rows(prompt_ref, parent_ref)
    rows = jnp.concatenate(pieces + shared, axis=0)
    out_ref[...] = rows.astype(BF16)
    wide_ref[...] = jnp.concatenate([rows, jnp.zeros_like(rows)], axis=0).astype(BF16)


def pack_kernel(fork_ref, prompt_ref, parent_ref, send_ref, table_ref):
    pieces, shared = shard_rows(prompt_ref, parent_ref)
    for p in range(parent_ref.shape[1]):
        table_ref[p] = jnp.concatenate(pieces[2 * p : 2 * p + 2] + shared, axis=0).astype(BF16)

    def place(d, carry):
        send_ref[d] = table_ref[fork_ref[d]]
        return carry

    lax.fori_loop(0, send_ref.shape[0], place, 0, unroll=min(8, send_ref.shape[0]))


def valid_keys(key, seg_rows, prompt_rows, counts, offsets, fork_ref, owner_ref, lengths_ref):
    n = owner_ref.shape[1]
    device = lax.axis_index("ctx")
    parent = fork_ref[device]
    place, row = jnp.full_like(key, -1), jnp.zeros_like(key)
    prompt = key < 0
    start, shard = 0, 0
    for count in counts:
        slot = key - start
        here = (slot >= 0) & (slot < count * seg_rows)
        place = jnp.where(here, shard + slot // seg_rows, place)
        row = jnp.where(here, slot % seg_rows, row)
        slot = slot - count * seg_rows
        here = (slot >= 0) & (slot < count * 2 * prompt_rows)
        prompt = prompt | (here & (slot % (2 * prompt_rows) < prompt_rows))
        start += count * (seg_rows + 2 * prompt_rows)
        shard += count
    block = place
    if offsets is not None:
        block = jnp.full_like(key, -1)
        for k in range(n):
            owner = device ^ jnp.where(device % 2 == 0, offsets[0][k], offsets[1][k])
            block = jnp.where(place == k, owner, block)

    def step(j, position):
        return jnp.where(block == owner_ref[parent, j], j * seg_rows + row, position)

    beyond = jnp.full_like(key, n * seg_rows)
    position = lax.fori_loop(0, n, step, beyond, unroll=min(16, n))
    return prompt | (position < lengths_ref[parent])


def split_keys(keys):
    keys = keys * (LOG2E * HD**-0.5)
    high = keys.astype(BF16)
    return jnp.concatenate([high, (keys - high.astype(F32)).astype(BF16)], axis=1)


def shard_keys(shards, seg_rows, prompt_rows, choice_ref, mask, fill, g):
    def rows(start, size):
        parts = [r[:, pl.ds(start, size), g * HD : (g + 1) * HD].astype(F32).reshape(-1, HD) for r in shards]
        return jnp.concatenate(parts, axis=0)

    def parent_rows(start):
        found = rows(start, seg_rows)
        for p in range(1, choice_ref.shape[0]):
            chosen = choice_ref[p, 0:1, :] > 0
            found = jnp.where(chosen, rows(start + p * 2 * seg_rows, seg_rows), found)
        return found

    prompt = rows(shards[0].shape[1] - 2 * prompt_rows, 2 * prompt_rows)
    keys = jnp.concatenate([parent_rows(0), prompt], axis=0)
    shifted = pltpu.roll(prompt, prompt.shape[0] - prompt_rows, 0)
    values = jnp.concatenate([parent_rows(seg_rows), shifted], axis=0)
    keys = split_keys(jnp.where(mask > 0, keys, fill))
    return keys, jnp.where(mask > 0, values, 0.0).astype(BF16)


def attend(q_ref, ready, causal, take, group, many):
    span, columns = q_ref.shape[1:]
    kept = {}

    def score(c):
        g = c * many // group
        if g not in kept:
            kept.clear()
            kept[g] = ready(g)
        keys, values = kept[g]
        query = jnp.concatenate([q_ref[0, :, i * HD : (i + 1) * HD] for i in range(c * many, (c + 1) * many)], axis=0)
        query = jnp.concatenate([query, query], axis=1)
        scores = lax.dot_general(keys, query, (((1,), (1,)), ((), ())), preferred_element_type=F32)
        if causal is not None:
            own = scores[:span] + causal
            scores = jnp.concatenate([own, scores[span:]], axis=0) if scores.shape[0] > span else own
        return scores, jnp.max(scores, axis=0, keepdims=True), values

    chunks = columns // HD // many
    made = score(0)
    for c in range(chunks):
        (scores, highest, values), made = made, score(c + 1) if c + 1 < chunks else None

        def weigh(top, scores=scores, values=values):
            weights = jnp.exp2(scores - top).astype(BF16)
            return jnp.dot(values, weights, preferred_element_type=F32)

        take(c, pl.ds(c * many * span, many * span), highest, weigh)


def load_kernel(sizes, *refs):
    ins, refs = refs[:5], refs[5:]
    q_ref, own_ref, choice_ref, *marks, raw_ref, fork_ref, owner_ref, lengths_ref, sems = refs
    tables = fork_ref, owner_ref, lengths_ref
    pairs = list(zip(ins, (*tables, raw_ref), strict=False))
    rows = q_ref.shape[1] // LOADS
    for k in range(LOADS):
        pairs.append((ins[4].at[:, pl.ds(k * rows, rows)], q_ref.at[:, pl.ds(k * rows, rows)]))
    copies = [pltpu.make_async_copy(src, dst, sems.at[k]) for k, (src, dst) in enumerate(pairs)]
    for copy in copies:
        copy.start()
    for copy in copies[:3]:
        copy.wait()
    parent = fork_ref[lax.axis_index("ctx")]
    for p in range(choice_ref.shape[0]):
        choice_ref[p] = jnp.full((8, HD), jnp.where(parent == p, 1.0, 0.0), F32)
    start = 0
    for across_ref, down_ref in zip(marks[::2], marks[1::2], strict=True):
        key = lax.broadcasted_iota(jnp.int32, (8, down_ref.shape[0]), 1)
        valid = valid_keys(key + start, *sizes, *tables).astype(F32)
        down_ref[...] = jnp.concatenate([valid] * (HD // 8), axis=0).T
        ahead = across_ref.shape[1] - down_ref.shape[0]
        if ahead:
            key = lax.broadcasted_iota(jnp.int32, (8, across_ref.shape[1]), 1) - ahead
            valid = ((key < 0) | valid_keys(key + start, *sizes, *tables)).astype(F32)
        across_ref[...] = jnp.concatenate([valid, valid], axis=0).astype(BF16)
        start += down_ref.shape[0]
    copies[3].wait()
    own_ref[...] = jnp.swapaxes(raw_ref[...], 0, 1)
    for copy in copies[4:]:
        copy.wait()


def near_kernel(seg_rows, prompt_rows, q_ref, own_ref, choice_ref, *refs):
    *others, state_ref, fill_ref = refs
    span = q_ref.shape[1]
    kv_heads = own_ref.shape[2] // HD
    group = q_ref.shape[2] // HD // kv_heads
    time = lax.broadcasted_iota(jnp.int32, (span, NEAR_HEADS * span), 1) % span
    causal = jnp.where(lax.broadcasted_iota(jnp.int32, time.shape, 0) <= time, 0.0, -jnp.inf)

    def ready(g):
        part = slice(g * HD, (g + 1) * HD)
        keys = own_ref[0, :, part].astype(F32)
        fill = keys[0:1]
        fill_ref[g] = jnp.broadcast_to(fill, (8, HD))
        keys, values = split_keys(keys), own_ref[1, :, part]
        if others:
            across_ref, down_ref, *shards = others
            more = shard_keys(shards, seg_rows, prompt_rows, choice_ref, down_ref[...], fill, g)
            keys, values = jnp.concatenate([keys, more[0]], axis=0), jnp.concatenate([values, more[1]], axis=0)
            ones = across_ref[...]
        else:
            ones = jnp.ones((16, span), BF16)
        return keys, jnp.concatenate([values.T, ones], axis=0)

    def take(c, lanes, highest, weigh):
        state_ref[: HD + 8, lanes] = weigh(highest)[: HD + 8]
        state_ref[HD + 8 :, lanes] = jnp.broadcast_to(highest, (8, highest.shape[1]))

    attend(q_ref, ready, causal, take, group, NEAR_HEADS)


def join_kernel(seg_rows, prompt_rows, final, q_ref, choice_ref, fill_ref, state_ref, across_ref, down_ref, *refs):
    kept, many = (3, LAST_HEADS) if final else (1, JOIN_HEADS)
    shards, refs = refs[:-kept], refs[-kept:]
    span, columns = q_ref.shape[1:]
    group = columns // HD // fill_ref.shape[0]
    copies = []

    def ready(g):
        keys, values = shard_keys(shards, seg_rows, prompt_rows, choice_ref, down_ref[...], fill_ref[g, 0:1], g)
        return keys, jnp.concatenate([values.T, across_ref[...]], axis=0)

    def take(c, lanes, highest, weigh):
        former = state_ref[HD + 8 :, lanes]
        top = jnp.maximum(former, highest)
        both = weigh(top[0:1])
        scale = jnp.exp2(former - top)
        total = state_ref[HD : HD + 8, lanes] * scale + both[HD : HD + 8]
        rows = (HD // 8, 8, -1)
        if not final:
            joined = state_ref[:HD, lanes].reshape(rows) * scale[None] + both[:HD].reshape(rows)
            refs[0][:HD, lanes] = joined.reshape(HD, -1)
            refs[0][HD : HD + 8, lanes] = total
            refs[0][HD + 8 :, lanes] = top
            return
        out_ref, stage, sems = refs
        share = 1.0 / total
        scale = scale * share
        result = state_ref[:HD, lanes].reshape(rows) * scale[None] + both[:HD].reshape(rows) * share[None]
        result = result.reshape(HD, -1).astype(BF16)
        for k in range(many):
            i = c * many + k
            stage[:, i * HD : (i + 1) * HD] = result[:, k * span : (k + 1) * span].T
            if (i + 1) % OUT_HEADS == 0:
                part = pl.ds((i + 1 - OUT_HEADS) * HD, OUT_HEADS * HD)
                copies.append(pltpu.make_async_copy(stage.at[:, part], out_ref.at[0, :, part], sems.at[len(copies)]))
                copies[-1].start()

    attend(q_ref, ready, None, take, group, many)
    for copy in copies:
        copy.wait()


def permute(x, target, n):
    return lax.ppermute(x, "ctx", [(i, target(i)) for i in range(n)])


def pair_steps(n):
    return range(n // 4 - 2, 0, -1)


def gather_shards(shard, both, n):
    far, near = n - 4, 2
    mate = permute(shard, lambda i: i ^ 1, n)
    first = permute(shard, lambda i: i ^ far, n)
    both = lax.dynamic_update_slice(both, mate, (shard.shape[0], 0))
    pairs = pair_steps(n)
    wide = [permute(both, lambda i, j=j: i ^ (2 * (2 * j + i % 2)), n) for j in pairs]
    side = permute(shard, lambda i: i ^ near, n)
    passed = permute(first, lambda i: i ^ near, n)
    soon = jnp.concatenate([*wide[1:], first, side], axis=0)
    late = jnp.concatenate([*wide[:1], passed], axis=0)
    soon_theirs = permute(soon, lambda i: i ^ 1, n)
    late_theirs = permute(late, lambda i: i ^ 1, n)
    straight, early = [far, near], []
    for core in range(2):
        steps = [[2 * (2 * j + core), 2 * (2 * j + core) ^ 1] for j in pairs]
        early.append(([o for step in steps[1:] for o in step], [*steps[0], far ^ near]))
    offsets = []
    for core in range(2):
        (mine, last), other = early[core], early[1 - core]
        theirs = [o ^ 1 for o in (*other[0], *straight)]
        offsets.append([0, 1, *straight, *mine, *theirs, *last, *[o ^ 1 for o in other[1]]])
    return [[shard, mate, first, side], [*wide[1:], soon_theirs, late], [late_theirs]], offsets


def use_gather(mesh_size, parents, seg_rows, prompt_rows):
    power = mesh_size >= 8 and mesh_size & (mesh_size - 1) == 0
    return power and parents * seg_rows + prompt_rows <= 2 * (seg_rows + prompt_rows)


def body(child_q, child_kv, prompt_kv, parent_kv, fork_list, owner_map, lengths):
    n = lax.axis_size("ctx")
    seg_rows, prompt_rows = parent_kv.shape[0], prompt_kv.shape[0]
    parents = parent_kv.shape[1]
    span, width = child_kv.shape[1], child_kv.shape[3]
    kv_heads = width // HD
    gather = use_gather(n, parents, seg_rows, prompt_rows)
    if gather:
        rows = 2 * (parents * seg_rows + prompt_rows)
        shard, both = pl.pallas_call(
            shard_kernel,
            out_shape=[jax.ShapeDtypeStruct((k * rows, width), BF16) for k in (1, 2)],
            in_specs=[HBM, HBM],
            out_specs=[VMEM, VMEM],
            scratch_shapes=[
                pltpu.VMEM(prompt_kv.shape, BF16),
                pltpu.VMEM(parent_kv.shape, BF16),
                pltpu.SemaphoreType.DMA((2,)),
            ],
            compiler_params=limit(2),
            name="shard",
        )(*in_hbm(prompt_kv, parent_kv))
        batches, offsets = gather_shards(shard, both, n)
    else:
        rows = 2 * (seg_rows + prompt_rows)
        send = pl.pallas_call(
            pack_kernel,
            out_shape=jax.ShapeDtypeStruct((n, rows, width), BF16),
            in_specs=[SMEM, VMEM, VMEM],
            out_specs=VMEM,
            scratch_shapes=[pltpu.VMEM((parents, rows, width), BF16)],
            name="pack",
        )(fork_list, prompt_kv, parent_kv)
        batches, offsets = [[], [lax.all_to_all(send, "ctx", split_axis=0, concat_axis=0, tiled=True)]], None
    batches = [[s.reshape(-1, rows, width) for s in batch] for batch in batches]
    counts = [sum(s.shape[0] for s in batch) for batch in batches]
    slots = seg_rows + 2 * prompt_rows
    heads = child_q.shape[2] // HD
    masks = []
    for k, count in enumerate(counts):
        if count:
            ahead = 0 if k else span
            masks += [((16, ahead + count * slots), BF16), ((count * slots, HD), F32)]
    query, own, choice, *marks = pl.pallas_call(
        functools.partial(load_kernel, (seg_rows, prompt_rows, counts, offsets)),
        out_shape=[
            jax.ShapeDtypeStruct(child_q.shape, BF16),
            jax.ShapeDtypeStruct((2, span, width), BF16),
            jax.ShapeDtypeStruct((parents if gather else 1, 8, HD), F32),
            *[jax.ShapeDtypeStruct(*mask) for mask in masks],
        ],
        in_specs=[HBM] * 5,
        out_specs=[VMEM] * (3 + len(masks)),
        scratch_shapes=[
            pltpu.VMEM(child_kv.shape[1:], BF16),
            *[pltpu.SMEM(x.shape, jnp.int32) for x in (fork_list, owner_map, lengths)],
            pltpu.SemaphoreType.DMA((4 + LOADS,)),
        ],
        compiler_params=limit(8),
        name="load",
    )(*in_hbm(fork_list, owner_map, lengths, child_kv[0], child_q))
    marks = [marks[2 * k : 2 * k + 2] for k in range(len(marks) // 2)]
    marks = [[]] * (len(counts) - len(marks)) + marks
    state_shape = jax.ShapeDtypeStruct((HD + 16, heads * span), F32)
    state, fill = pl.pallas_call(
        functools.partial(near_kernel, seg_rows, prompt_rows),
        out_shape=[state_shape, jax.ShapeDtypeStruct((kv_heads, 8, HD), F32)],
        in_specs=[VMEM] * (3 + len(marks[0]) + len(batches[0])),
        out_specs=[VMEM] * 2,
        compiler_params=limit(16),
        name="near",
    )(query, own, choice, *marks[0], *batches[0])
    for k in range(1, len(batches)):
        final = k == len(batches) - 1
        state = pl.pallas_call(
            functools.partial(join_kernel, seg_rows, prompt_rows, final),
            out_shape=jax.ShapeDtypeStruct(child_q.shape, BF16) if final else state_shape,
            in_specs=[VMEM] * (6 + len(batches[k])),
            out_specs=HBM if final else VMEM,
            scratch_shapes=[
                pltpu.VMEM(child_q.shape[1:], BF16),
                pltpu.SemaphoreType.DMA((heads // OUT_HEADS,)),
            ][: 2 * final],
            compiler_params=limit(16 if gather else 48),
        )(query, choice, fill, state, *marks[k], *batches[k])
    return state


def solution(mesh):
    placed = (
        P(("groups", "ctx"), None, None),
        P(("groups", "ctx"), None, None, None),
        P(("groups", "ctx"), None, None),
        P(("groups", "ctx"), None, None, None),
        P("groups"),
        P("groups", None),
        P("groups"),
    )
    return jax.shard_map(
        body,
        mesh=mesh,
        in_specs=placed,
        out_specs=P(("groups", "ctx"), None, None),
        check_vma=False,
    )
```

```python
import functools

import jax
import jax.numpy as jnp
from jax import lax
from jax.experimental import pallas as pl
from jax.experimental.pallas import tpu as pltpu
from jax.sharding import PartitionSpec as P

HD = 128
LOG2E = 1.4426950408889634
F32 = jnp.float32
BF16 = jnp.bfloat16
NEAR_HEADS, LAST_HEADS, OUT_HEADS, LOADS = 8, 8, 8, 4
VMEM = pl.BlockSpec(memory_space=pltpu.VMEM)
SMEM = pl.BlockSpec(memory_space=pltpu.SMEM)
HBM = pl.BlockSpec(memory_space=pltpu.HBM)


def in_hbm(*arrays):
    return [pltpu.with_memory_space_constraint(x, pltpu.HBM) for x in arrays]


def limit(mib):
    return pltpu.CompilerParams(vmem_limit_bytes=mib << 20)


def shard_rows(prompt_ref, parent_ref):
    prompt = prompt_ref[...].astype(F32)
    rows = []
    for p in range(parent_ref.shape[1]):
        piece = parent_ref[:, p].astype(F32)
        rows += [piece[:, 0, :], piece[:, 1, :]]
    return rows, [prompt[:, 0, :], prompt[:, 1, :]]


def shard_kernel(prompt_hbm, parent_hbm, out_ref, wide_ref, prompt_ref, parent_ref, sems):
    copies = [
        pltpu.make_async_copy(parent_hbm, parent_ref, sems.at[0]),
        pltpu.make_async_copy(prompt_hbm, prompt_ref, sems.at[1]),
    ]
    for copy in copies:
        copy.start()
    for copy in copies:
        copy.wait()
    pieces, shared = shard_rows(prompt_ref, parent_ref)
    rows = jnp.concatenate(pieces + shared, axis=0)
    out_ref[...] = rows.astype(BF16)
    wide_ref[...] = jnp.concatenate([rows, jnp.zeros_like(rows)], axis=0).astype(BF16)


def pack_kernel(fork_ref, prompt_ref, parent_ref, send_ref, table_ref):
    pieces, shared = shard_rows(prompt_ref, parent_ref)
    for p in range(parent_ref.shape[1]):
        table_ref[p] = jnp.concatenate(pieces[2 * p : 2 * p + 2] + shared, axis=0).astype(BF16)

    def place(d, carry):
        send_ref[d] = table_ref[fork_ref[d]]
        return carry

    lax.fori_loop(0, send_ref.shape[0], place, 0, unroll=min(8, send_ref.shape[0]))


def valid_keys(key, seg_rows, prompt_rows, counts, offsets, fork_ref, owner_ref, lengths_ref):
    n = owner_ref.shape[1]
    device = lax.axis_index("ctx")
    parent = fork_ref[device]
    place, row = jnp.full_like(key, -1), jnp.zeros_like(key)
    prompt = key < 0
    start, shard = 0, 0
    for count in counts:
        slot = key - start
        here = (slot >= 0) & (slot < count * seg_rows)
        place = jnp.where(here, shard + slot // seg_rows, place)
        row = jnp.where(here, slot % seg_rows, row)
        slot = slot - count * seg_rows
        here = (slot >= 0) & (slot < count * 2 * prompt_rows)
        prompt = prompt | (here & (slot % (2 * prompt_rows) < prompt_rows))
        start += count * (seg_rows + 2 * prompt_rows)
        shard += count
    block = place
    if offsets is not None:
        block = jnp.full_like(key, -1)
        for k in range(n):
            owner = device ^ jnp.where(device % 2 == 0, offsets[0][k], offsets[1][k])
            block = jnp.where(place == k, owner, block)

    def step(j, position):
        return jnp.where(block == owner_ref[parent, j], j * seg_rows + row, position)

    beyond = jnp.full_like(key, n * seg_rows)
    position = lax.fori_loop(0, n, step, beyond, unroll=min(16, n))
    return prompt | (position < lengths_ref[parent])


def split_keys(keys):
    keys = keys * (LOG2E * HD**-0.5)
    high = keys.astype(BF16)
    return jnp.concatenate([high, (keys - high.astype(F32)).astype(BF16)], axis=1)


def shard_keys(shards, seg_rows, prompt_rows, choice_ref, mask, fill, g):
    def rows(start, size):
        parts = [r[:, pl.ds(start, size), g * HD : (g + 1) * HD].astype(F32).reshape(-1, HD) for r in shards]
        return jnp.concatenate(parts, axis=0)

    def parent_rows(start):
        found = rows(start, seg_rows)
        for p in range(1, choice_ref.shape[0]):
            chosen = choice_ref[p, 0:1, :] > 0
            found = jnp.where(chosen, rows(start + p * 2 * seg_rows, seg_rows), found)
        return found

    prompt = rows(shards[0].shape[1] - 2 * prompt_rows, 2 * prompt_rows)
    keys = jnp.concatenate([parent_rows(0), prompt], axis=0)
    shifted = pltpu.roll(prompt, prompt.shape[0] - prompt_rows, 0)
    values = jnp.concatenate([parent_rows(seg_rows), shifted], axis=0)
    keys = split_keys(jnp.where(mask > 0, keys, fill))
    return keys, jnp.where(mask > 0, values, 0.0).astype(BF16)


def attend(q_ref, ready, causal, take, group, many):
    span, columns = q_ref.shape[1:]
    kept = {}

    def score(c):
        g = c * many // group
        if g not in kept:
            kept.clear()
            kept[g] = ready(g)
        keys, values = kept[g]
        query = jnp.concatenate([q_ref[0, :, i * HD : (i + 1) * HD] for i in range(c * many, (c + 1) * many)], axis=0)
        query = jnp.concatenate([query, query], axis=1)
        scores = lax.dot_general(keys, query, (((1,), (1,)), ((), ())), preferred_element_type=F32)
        if causal is not None:
            own = scores[:span] + causal
            scores = jnp.concatenate([own, scores[span:]], axis=0) if scores.shape[0] > span else own
        return scores, jnp.max(scores, axis=0, keepdims=True), values

    chunks = columns // HD // many
    made = score(0)
    for c in range(chunks):
        (scores, highest, values), made = made, score(c + 1) if c + 1 < chunks else None

        def weigh(top, scores=scores, values=values):
            weights = jnp.exp2(scores - top).astype(BF16)
            return jnp.dot(values, weights, preferred_element_type=F32)

        take(c, pl.ds(c * many * span, many * span), highest, weigh)


def load_kernel(sizes, *refs):
    ins, refs = refs[:5], refs[5:]
    q_ref, own_ref, choice_ref, *marks, raw_ref, fork_ref, owner_ref, lengths_ref, sems = refs
    tables = fork_ref, owner_ref, lengths_ref
    pairs = list(zip(ins, (*tables, raw_ref), strict=False))
    rows = q_ref.shape[1] // LOADS
    for k in range(LOADS):
        pairs.append((ins[4].at[:, pl.ds(k * rows, rows)], q_ref.at[:, pl.ds(k * rows, rows)]))
    copies = [pltpu.make_async_copy(src, dst, sems.at[k]) for k, (src, dst) in enumerate(pairs)]
    for copy in copies:
        copy.start()
    for copy in copies[:3]:
        copy.wait()
    parent = fork_ref[lax.axis_index("ctx")]
    for p in range(choice_ref.shape[0]):
        choice_ref[p] = jnp.full((8, HD), jnp.where(parent == p, 1.0, 0.0), F32)
    start = 0
    for across_ref, down_ref in zip(marks[::2], marks[1::2], strict=True):
        key = lax.broadcasted_iota(jnp.int32, (8, down_ref.shape[0]), 1)
        valid = valid_keys(key + start, *sizes, *tables).astype(F32)
        down_ref[...] = jnp.concatenate([valid] * (HD // 8), axis=0).T
        ahead = across_ref.shape[1] - down_ref.shape[0]
        if ahead:
            key = lax.broadcasted_iota(jnp.int32, (8, across_ref.shape[1]), 1) - ahead
            valid = ((key < 0) | valid_keys(key + start, *sizes, *tables)).astype(F32)
        across_ref[...] = jnp.concatenate([valid, valid], axis=0).astype(BF16)
        start += down_ref.shape[0]
    copies[3].wait()
    own_ref[...] = jnp.swapaxes(raw_ref[...], 0, 1)
    for copy in copies[4:]:
        copy.wait()


def near_kernel(seg_rows, prompt_rows, q_ref, own_ref, choice_ref, *refs):
    *others, state_ref, fill_ref = refs
    span = q_ref.shape[1]
    kv_heads = own_ref.shape[2] // HD
    group = q_ref.shape[2] // HD // kv_heads
    time = lax.broadcasted_iota(jnp.int32, (span, NEAR_HEADS * span), 1) % span
    causal = jnp.where(lax.broadcasted_iota(jnp.int32, time.shape, 0) <= time, 0.0, -jnp.inf)

    def ready(g):
        part = slice(g * HD, (g + 1) * HD)
        keys = own_ref[0, :, part].astype(F32)
        fill = keys[0:1]
        fill_ref[g] = jnp.broadcast_to(fill, (8, HD))
        keys, values = split_keys(keys), own_ref[1, :, part]
        if others:
            across_ref, down_ref, *shards = others
            more = shard_keys(shards, seg_rows, prompt_rows, choice_ref, down_ref[...], fill, g)
            keys, values = jnp.concatenate([keys, more[0]], axis=0), jnp.concatenate([values, more[1]], axis=0)
            ones = across_ref[...]
        else:
            ones = jnp.ones((16, span), BF16)
        return keys, jnp.concatenate([values.T, ones], axis=0)

    def take(c, lanes, highest, weigh):
        state_ref[: HD + 8, lanes] = weigh(highest)[: HD + 8]
        state_ref[HD + 8 :, lanes] = jnp.broadcast_to(highest, (8, highest.shape[1]))

    attend(q_ref, ready, causal, take, group, NEAR_HEADS)


def ready_kernel(seg_rows, prompt_rows, start, choice_ref, fill_ref, down_ref, *refs):
    *shards, keys_ref, values_ref = refs
    for g in range(fill_ref.shape[0]):
        mask = down_ref[start : start + keys_ref.shape[1]]
        made = shard_keys(shards, seg_rows, prompt_rows, choice_ref, mask, fill_ref[g, 0:1], g)
        keys_ref[g], values_ref[g] = made


def join_kernel(seg_rows, prompt_rows, count, q_ref, choice_ref, fill_ref, state_ref, across_ref, down_ref, *refs):
    shards, (*made_refs, out_ref, stage, sems) = refs[:count], refs[count:]
    many = LAST_HEADS
    span, columns = q_ref.shape[1:]
    group = columns // HD // fill_ref.shape[0]
    copies = []

    def ready(g):
        known = sum(r.shape[1] for r in made_refs[::2])
        keys, values = shard_keys(shards, seg_rows, prompt_rows, choice_ref, down_ref[known:], fill_ref[g, 0:1], g)
        if made_refs:
            keys = jnp.concatenate([*[r[g] for r in made_refs[::2]], keys], axis=0)
            values = jnp.concatenate([*[r[g] for r in made_refs[1::2]], values], axis=0)
        return keys, jnp.concatenate([values.T, across_ref[...]], axis=0)

    def take(c, lanes, highest, weigh):
        former = state_ref[HD + 8 :, lanes]
        top = jnp.maximum(former, highest)
        both = weigh(top[0:1])
        scale = jnp.exp2(former - top)
        total = state_ref[HD : HD + 8, lanes] * scale + both[HD : HD + 8]
        rows = (HD // 8, 8, -1)
        share = 1.0 / total
        scale = scale * share
        result = state_ref[:HD, lanes].reshape(rows) * scale[None] + both[:HD].reshape(rows) * share[None]
        result = result.reshape(HD, -1).astype(BF16)
        for k in range(many):
            i = c * many + k
            stage[:, i * HD : (i + 1) * HD] = result[:, k * span : (k + 1) * span].T
            if (i + 1) % OUT_HEADS == 0:
                part = pl.ds((i + 1 - OUT_HEADS) * HD, OUT_HEADS * HD)
                copies.append(pltpu.make_async_copy(stage.at[:, part], out_ref.at[0, :, part], sems.at[len(copies)]))
                copies[-1].start()

    attend(q_ref, ready, None, take, group, many)
    for copy in copies:
        copy.wait()


def permute(x, target, n):
    return lax.ppermute(x, "ctx", [(i, target(i)) for i in range(n)])


def pair_steps(n):
    return range(n // 4 - 2, 0, -1)


def gather_shards(shard, both, n):
    far, near = n - 4, 2
    mate = permute(shard, lambda i: i ^ 1, n)
    first = permute(shard, lambda i: i ^ far, n)
    both = lax.dynamic_update_slice(both, mate, (shard.shape[0], 0))
    pairs = pair_steps(n)
    wide = [permute(both, lambda i, j=j: i ^ (2 * (2 * j + i % 2)), n) for j in pairs]
    side = permute(shard, lambda i: i ^ near, n)
    passed = permute(first, lambda i: i ^ near, n)
    early = jnp.concatenate([first, side], axis=0)
    late = jnp.concatenate([*wide, passed], axis=0)
    early_theirs = permute(early, lambda i: i ^ 1, n)
    late_theirs = permute(late, lambda i: i ^ 1, n)
    straight, got = [far, near], []
    for core in range(2):
        steps = [2 * (2 * j + core) for j in pairs]
        got.append([*[o for d in steps for o in (d, d ^ 1)], far ^ near])
    close = [0, 1, *straight, *[o ^ 1 for o in straight]]
    offsets = [[*close, *got[core], *[o ^ 1 for o in got[1 - core]]] for core in range(2)]
    return [[shard, mate, early, early_theirs], [late], [late_theirs]], offsets


def use_gather(mesh_size, parents, seg_rows, prompt_rows):
    power = mesh_size >= 8 and mesh_size & (mesh_size - 1) == 0
    return power and parents * seg_rows + prompt_rows <= 2 * (seg_rows + prompt_rows)


def body(child_q, child_kv, prompt_kv, parent_kv, fork_list, owner_map, lengths):
    n = lax.axis_size("ctx")
    seg_rows, prompt_rows = parent_kv.shape[0], prompt_kv.shape[0]
    parents = parent_kv.shape[1]
    span, width = child_kv.shape[1], child_kv.shape[3]
    kv_heads = width // HD
    gather = use_gather(n, parents, seg_rows, prompt_rows)
    if gather:
        rows = 2 * (parents * seg_rows + prompt_rows)
        shard, both = pl.pallas_call(
            shard_kernel,
            out_shape=[jax.ShapeDtypeStruct((k * rows, width), BF16) for k in (1, 2)],
            in_specs=[HBM, HBM],
            out_specs=[VMEM, VMEM],
            scratch_shapes=[
                pltpu.VMEM(prompt_kv.shape, BF16),
                pltpu.VMEM(parent_kv.shape, BF16),
                pltpu.SemaphoreType.DMA((2,)),
            ],
            compiler_params=limit(2),
            name="shard",
        )(*in_hbm(prompt_kv, parent_kv))
        batches, offsets = gather_shards(shard, both, n)
    else:
        rows = 2 * (seg_rows + prompt_rows)
        send = pl.pallas_call(
            pack_kernel,
            out_shape=jax.ShapeDtypeStruct((n, rows, width), BF16),
            in_specs=[SMEM, VMEM, VMEM],
            out_specs=VMEM,
            scratch_shapes=[pltpu.VMEM((parents, rows, width), BF16)],
            name="pack",
        )(fork_list, prompt_kv, parent_kv)
        batches, offsets = [[], [lax.all_to_all(send, "ctx", split_axis=0, concat_axis=0, tiled=True)]], None
    batches = [[s.reshape(-1, rows, width) for s in batch] for batch in batches]
    sizes = [sum(s.shape[0] for s in batch) for batch in batches]
    counts = [sizes[0], sum(sizes[1:])]
    slots = seg_rows + 2 * prompt_rows
    heads = child_q.shape[2] // HD
    masks = []
    for k, count in enumerate(counts):
        if count:
            ahead = 0 if k else span
            masks += [((16, ahead + count * slots), BF16), ((count * slots, HD), F32)]
    query, own, choice, *marks = pl.pallas_call(
        functools.partial(load_kernel, (seg_rows, prompt_rows, sizes, offsets)),
        out_shape=[
            jax.ShapeDtypeStruct(child_q.shape, BF16),
            jax.ShapeDtypeStruct((2, span, width), BF16),
            jax.ShapeDtypeStruct((parents if gather else 1, 8, HD), F32),
            *[jax.ShapeDtypeStruct(*mask) for mask in masks],
        ],
        in_specs=[HBM] * 5,
        out_specs=[VMEM] * (3 + len(masks)),
        scratch_shapes=[
            pltpu.VMEM(child_kv.shape[1:], BF16),
            *[pltpu.SMEM(x.shape, jnp.int32) for x in (fork_list, owner_map, lengths)],
            pltpu.SemaphoreType.DMA((4 + LOADS,)),
        ],
        compiler_params=limit(8),
        name="load",
    )(*in_hbm(fork_list, owner_map, lengths, child_kv[0], child_q))
    marks = [marks[2 * k : 2 * k + 2] for k in range(len(marks) // 2)]
    marks = [[]] * (len(counts) - len(marks)) + marks
    state_shape = jax.ShapeDtypeStruct((HD + 16, heads * span), F32)
    state, fill = pl.pallas_call(
        functools.partial(near_kernel, seg_rows, prompt_rows),
        out_shape=[state_shape, jax.ShapeDtypeStruct((kv_heads, 8, HD), F32)],
        in_specs=[VMEM] * (3 + len(marks[0]) + len(batches[0])),
        out_specs=[VMEM] * 2,
        compiler_params=limit(16),
        name="near",
    )(query, own, choice, *marks[0], *batches[0])
    made = []
    for k in range(1, len(batches) - 1):
        made += pl.pallas_call(
            functools.partial(ready_kernel, seg_rows, prompt_rows, sum(sizes[1:k]) * slots),
            out_shape=[jax.ShapeDtypeStruct((kv_heads, sizes[k] * slots, m * HD), BF16) for m in (2, 1)],
            in_specs=[VMEM] * (3 + len(batches[k])),
            out_specs=[VMEM] * 2,
            compiler_params=limit(4),
        )(choice, fill, marks[1][1], *batches[k])
    last = batches[-1]
    return pl.pallas_call(
        functools.partial(join_kernel, seg_rows, prompt_rows, len(last)),
        out_shape=jax.ShapeDtypeStruct(child_q.shape, BF16),
        in_specs=[VMEM] * (6 + len(last) + len(made)),
        out_specs=HBM,
        scratch_shapes=[pltpu.VMEM(child_q.shape[1:], BF16), pltpu.SemaphoreType.DMA((heads // OUT_HEADS,))],
        compiler_params=limit(16 if gather else 48),
        name="join",
    )(query, choice, fill, state, *marks[1], *last, *made)


def solution(mesh):
    placed = (
        P(("groups", "ctx"), None, None),
        P(("groups", "ctx"), None, None, None),
        P(("groups", "ctx"), None, None),
        P(("groups", "ctx"), None, None, None),
        P("groups"),
        P("groups", None),
        P("groups"),
    )
    return jax.shard_map(
        body,
        mesh=mesh,
        in_specs=placed,
        out_specs=P(("groups", "ctx"), None, None),
        check_vma=False,
    )
```

```python
import functools

import jax
import jax.numpy as jnp
from jax import lax
from jax.experimental import pallas as pl
from jax.experimental.pallas import tpu as pltpu
from jax.sharding import PartitionSpec as P

HD = 128
LOG2E = 1.4426950408889634
F32 = jnp.float32
BF16 = jnp.bfloat16
NEAR_HEADS, LAST_HEADS, OUT_HEADS, LOADS = 8, 8, 8, 1
VMEM = pl.BlockSpec(memory_space=pltpu.VMEM)
SMEM = pl.BlockSpec(memory_space=pltpu.SMEM)
HBM = pl.BlockSpec(memory_space=pltpu.HBM)


def in_hbm(*arrays):
    return [pltpu.with_memory_space_constraint(x, pltpu.HBM) for x in arrays]


def limit(mib):
    return pltpu.CompilerParams(vmem_limit_bytes=mib << 20)


def shard_rows(prompt_ref, parent_ref):
    prompt = prompt_ref[...].astype(F32)
    rows = []
    for p in range(parent_ref.shape[1]):
        piece = parent_ref[:, p].astype(F32)
        rows += [piece[:, 0, :], piece[:, 1, :]]
    return rows, [prompt[:, 0, :], prompt[:, 1, :]]


def shard_kernel(prompt_hbm, parent_hbm, out_ref, wide_ref, prompt_ref, parent_ref, sems):
    copies = [
        pltpu.make_async_copy(parent_hbm, parent_ref, sems.at[0]),
        pltpu.make_async_copy(prompt_hbm, prompt_ref, sems.at[1]),
    ]
    for copy in copies:
        copy.start()
    for copy in copies:
        copy.wait()
    pieces, shared = shard_rows(prompt_ref, parent_ref)
    rows = jnp.concatenate(pieces + shared, axis=0)
    out_ref[...] = rows.astype(BF16)
    wide_ref[...] = jnp.concatenate([rows, jnp.zeros_like(rows)], axis=0).astype(BF16)


def pack_kernel(fork_ref, prompt_ref, parent_ref, send_ref, table_ref):
    pieces, shared = shard_rows(prompt_ref, parent_ref)
    for p in range(parent_ref.shape[1]):
        table_ref[p] = jnp.concatenate(pieces[2 * p : 2 * p + 2] + shared, axis=0).astype(BF16)

    def place(d, carry):
        send_ref[d] = table_ref[fork_ref[d]]
        return carry

    lax.fori_loop(0, send_ref.shape[0], place, 0, unroll=min(8, send_ref.shape[0]))


def valid_keys(key, seg_rows, prompt_rows, counts, offsets, fork_ref, owner_ref, lengths_ref):
    n = owner_ref.shape[1]
    device = lax.axis_index("ctx")
    parent = fork_ref[device]
    place, row = jnp.full_like(key, -1), jnp.zeros_like(key)
    prompt = key < 0
    start, shard = 0, 0
    for count in counts:
        slot = key - start
        here = (slot >= 0) & (slot < count * seg_rows)
        place = jnp.where(here, shard + slot // seg_rows, place)
        row = jnp.where(here, slot % seg_rows, row)
        slot = slot - count * seg_rows
        here = (slot >= 0) & (slot < count * 2 * prompt_rows)
        prompt = prompt | (here & (slot % (2 * prompt_rows) < prompt_rows))
        start += count * (seg_rows + 2 * prompt_rows)
        shard += count
    block = place
    if offsets is not None:
        block = jnp.full_like(key, -1)
        for k in range(n):
            owner = device ^ jnp.where(device % 2 == 0, offsets[0][k], offsets[1][k])
            block = jnp.where(place == k, owner, block)

    def step(j, position):
        return jnp.where(block == owner_ref[parent, j], j * seg_rows + row, position)

    beyond = jnp.full_like(key, n * seg_rows)
    position = lax.fori_loop(0, n, step, beyond, unroll=min(16, n))
    return prompt | (position < lengths_ref[parent])


def split_keys(keys):
    keys = keys * (LOG2E * HD**-0.5)
    high = keys.astype(BF16)
    return jnp.concatenate([high, (keys - high.astype(F32)).astype(BF16)], axis=1)


def shard_keys(shards, seg_rows, prompt_rows, choice_ref, mask, fill, g):
    def rows(start, size):
        parts = [r[:, pl.ds(start, size), g * HD : (g + 1) * HD].astype(F32).reshape(-1, HD) for r in shards]
        return jnp.concatenate(parts, axis=0)

    def parent_rows(start):
        found = rows(start, seg_rows)
        for p in range(1, choice_ref.shape[0]):
            chosen = choice_ref[p, 0:1, :] > 0
            found = jnp.where(chosen, rows(start + p * 2 * seg_rows, seg_rows), found)
        return found

    prompt = rows(shards[0].shape[1] - 2 * prompt_rows, 2 * prompt_rows)
    keys = jnp.concatenate([parent_rows(0), prompt], axis=0)
    shifted = pltpu.roll(prompt, prompt.shape[0] - prompt_rows, 0)
    values = jnp.concatenate([parent_rows(seg_rows), shifted], axis=0)
    keys = split_keys(jnp.where(mask > 0, keys, fill))
    return keys, jnp.where(mask > 0, values, 0.0).astype(BF16)


def attend(q_ref, ready, causal, take, group, many):
    span, columns = q_ref.shape[1:]
    kept = {}

    def score(c):
        g = c * many // group
        if g not in kept:
            kept.clear()
            kept[g] = ready(g)
        keys, values = kept[g]
        query = jnp.concatenate([q_ref[0, :, i * HD : (i + 1) * HD] for i in range(c * many, (c + 1) * many)], axis=0)
        query = jnp.concatenate([query, query], axis=1)
        scores = lax.dot_general(keys, query, (((1,), (1,)), ((), ())), preferred_element_type=F32)
        if causal is not None:
            own = scores[:span] + causal
            scores = jnp.concatenate([own, scores[span:]], axis=0) if scores.shape[0] > span else own
        return scores, jnp.max(scores, axis=0, keepdims=True), values

    chunks = columns // HD // many
    made = score(0)
    for c in range(chunks):
        (scores, highest, values), made = made, score(c + 1) if c + 1 < chunks else None

        def weigh(top, scores=scores, values=values):
            weights = jnp.exp2(scores - top).astype(BF16)
            return jnp.dot(values, weights, preferred_element_type=F32)

        take(c, pl.ds(c * many * span, many * span), highest, weigh)


def load_kernel(sizes, *refs):
    ins, refs = refs[:5], refs[5:]
    q_ref, own_ref, choice_ref, *marks, raw_ref, fork_ref, owner_ref, lengths_ref, sems = refs
    tables = fork_ref, owner_ref, lengths_ref
    pairs = list(zip(ins, (*tables, raw_ref), strict=False))
    rows = q_ref.shape[1] // LOADS
    for k in range(LOADS):
        pairs.append((ins[4].at[:, pl.ds(k * rows, rows)], q_ref.at[:, pl.ds(k * rows, rows)]))
    copies = [pltpu.make_async_copy(src, dst, sems.at[k]) for k, (src, dst) in enumerate(pairs)]
    for copy in copies:
        copy.start()
    for copy in copies[:3]:
        copy.wait()
    parent = fork_ref[lax.axis_index("ctx")]
    for p in range(choice_ref.shape[0]):
        choice_ref[p] = jnp.full((8, HD), jnp.where(parent == p, 1.0, 0.0), F32)
    start = 0
    for across_ref, down_ref in zip(marks[::2], marks[1::2], strict=True):
        key = lax.broadcasted_iota(jnp.int32, (8, down_ref.shape[0]), 1)
        valid = valid_keys(key + start, *sizes, *tables).astype(F32)
        down_ref[...] = jnp.concatenate([valid] * (HD // 8), axis=0).T
        ahead = across_ref.shape[1] - down_ref.shape[0]
        if ahead:
            key = lax.broadcasted_iota(jnp.int32, (8, across_ref.shape[1]), 1) - ahead
            valid = ((key < 0) | valid_keys(key + start, *sizes, *tables)).astype(F32)
        across_ref[...] = jnp.concatenate([valid, valid], axis=0).astype(BF16)
        start += down_ref.shape[0]
    copies[3].wait()
    own_ref[...] = jnp.swapaxes(raw_ref[...], 0, 1)
    for copy in copies[4:]:
        copy.wait()


def near_kernel(seg_rows, prompt_rows, q_ref, own_ref, choice_ref, *refs):
    *others, state_ref, fill_ref = refs
    span = q_ref.shape[1]
    kv_heads = own_ref.shape[2] // HD
    group = q_ref.shape[2] // HD // kv_heads
    time = lax.broadcasted_iota(jnp.int32, (span, NEAR_HEADS * span), 1) % span
    causal = jnp.where(lax.broadcasted_iota(jnp.int32, time.shape, 0) <= time, 0.0, -jnp.inf)

    def ready(g):
        part = slice(g * HD, (g + 1) * HD)
        keys = own_ref[0, :, part].astype(F32)
        fill = keys[0:1]
        fill_ref[g] = jnp.broadcast_to(fill, (8, HD))
        keys, values = split_keys(keys), own_ref[1, :, part]
        if others:
            across_ref, down_ref, *shards = others
            more = shard_keys(shards, seg_rows, prompt_rows, choice_ref, down_ref[...], fill, g)
            keys, values = jnp.concatenate([keys, more[0]], axis=0), jnp.concatenate([values, more[1]], axis=0)
            ones = across_ref[...]
        else:
            ones = jnp.ones((16, span), BF16)
        return keys, jnp.concatenate([values.T, ones], axis=0)

    def take(c, lanes, highest, weigh):
        state_ref[: HD + 8, lanes] = weigh(highest)[: HD + 8]
        state_ref[HD + 8 :, lanes] = jnp.broadcast_to(highest, (8, highest.shape[1]))

    attend(q_ref, ready, causal, take, group, NEAR_HEADS)


def ready_kernel(seg_rows, prompt_rows, start, choice_ref, fill_ref, down_ref, *refs):
    *shards, keys_ref, values_ref = refs
    for g in range(fill_ref.shape[0]):
        mask = down_ref[start : start + keys_ref.shape[1]]
        made = shard_keys(shards, seg_rows, prompt_rows, choice_ref, mask, fill_ref[g, 0:1], g)
        keys_ref[g], values_ref[g] = made


def join_kernel(seg_rows, prompt_rows, count, q_ref, choice_ref, fill_ref, state_ref, across_ref, down_ref, *refs):
    shards, (*made_refs, out_ref, stage, sems) = refs[:count], refs[count:]
    many = LAST_HEADS
    span, columns = q_ref.shape[1:]
    group = columns // HD // fill_ref.shape[0]
    copies = []

    def ready(g):
        known = sum(r.shape[1] for r in made_refs[::2])
        keys, values = shard_keys(shards, seg_rows, prompt_rows, choice_ref, down_ref[known:], fill_ref[g, 0:1], g)
        if made_refs:
            keys = jnp.concatenate([*[r[g] for r in made_refs[::2]], keys], axis=0)
            values = jnp.concatenate([*[r[g] for r in made_refs[1::2]], values], axis=0)
        return keys, jnp.concatenate([values.T, across_ref[...]], axis=0)

    def take(c, lanes, highest, weigh):
        former = state_ref[HD + 8 :, lanes]
        top = jnp.maximum(former, highest)
        both = weigh(top[0:1])
        scale = jnp.exp2(former - top)
        total = state_ref[HD : HD + 8, lanes] * scale + both[HD : HD + 8]
        rows = (HD // 8, 8, -1)
        share = 1.0 / total
        scale = scale * share
        result = state_ref[:HD, lanes].reshape(rows) * scale[None] + both[:HD].reshape(rows) * share[None]
        result = result.reshape(HD, -1).astype(BF16)
        for k in range(many):
            i = c * many + k
            stage[:, i * HD : (i + 1) * HD] = result[:, k * span : (k + 1) * span].T
            if (i + 1) % OUT_HEADS == 0:
                part = pl.ds((i + 1 - OUT_HEADS) * HD, OUT_HEADS * HD)
                copies.append(pltpu.make_async_copy(stage.at[:, part], out_ref.at[0, :, part], sems.at[len(copies)]))
                copies[-1].start()

    attend(q_ref, ready, None, take, group, many)
    for copy in copies:
        copy.wait()


def permute(x, target, n):
    return lax.ppermute(x, "ctx", [(i, target(i)) for i in range(n)])


def pair_steps(n):
    return range(n // 4 - 2, 0, -1)


def gather_shards(shard, both, n):
    far, near = n - 4, 2
    mate = permute(shard, lambda i: i ^ 1, n)
    first = permute(shard, lambda i: i ^ far, n)
    both = lax.dynamic_update_slice(both, mate, (shard.shape[0], 0))
    pairs = pair_steps(n)
    wide = [permute(both, lambda i, j=j: i ^ (2 * (2 * j + i % 2)), n) for j in pairs]
    side = permute(shard, lambda i: i ^ near, n)
    passed = permute(first, lambda i: i ^ near, n)
    early = jnp.concatenate([first, side], axis=0)
    soon = jnp.concatenate(wide[1:], axis=0)
    late = jnp.concatenate([*wide[:1], passed], axis=0)
    early_theirs = permute(early, lambda i: i ^ 1, n)
    soon_theirs = permute(soon, lambda i: i ^ 1, n)
    late_theirs = permute(late, lambda i: i ^ 1, n)
    straight, got = [far, near], []
    for core in range(2):
        steps = [[2 * (2 * j + core), 2 * (2 * j + core) ^ 1] for j in pairs]
        got.append(([o for step in steps[1:] for o in step], [*steps[0], far ^ near]))
    offsets = []
    for core in range(2):
        close = [0, 1, *straight, *[o ^ 1 for o in straight]]
        others = [[o ^ 1 for o in part] for part in got[1 - core]]
        offsets.append([*close, *got[core][0], *others[0], *got[core][1], *others[1]])
    return [[shard, mate, early, early_theirs], [soon], [soon_theirs, late], [late_theirs]], offsets


def use_gather(mesh_size, parents, seg_rows, prompt_rows):
    power = mesh_size >= 8 and mesh_size & (mesh_size - 1) == 0
    return power and parents * seg_rows + prompt_rows <= 2 * (seg_rows + prompt_rows)


def body(child_q, child_kv, prompt_kv, parent_kv, fork_list, owner_map, lengths):
    n = lax.axis_size("ctx")
    seg_rows, prompt_rows = parent_kv.shape[0], prompt_kv.shape[0]
    parents = parent_kv.shape[1]
    span, width = child_kv.shape[1], child_kv.shape[3]
    kv_heads = width // HD
    gather = use_gather(n, parents, seg_rows, prompt_rows)
    if gather:
        rows = 2 * (parents * seg_rows + prompt_rows)
        shard, both = pl.pallas_call(
            shard_kernel,
            out_shape=[jax.ShapeDtypeStruct((k * rows, width), BF16) for k in (1, 2)],
            in_specs=[HBM, HBM],
            out_specs=[VMEM, VMEM],
            scratch_shapes=[
                pltpu.VMEM(prompt_kv.shape, BF16),
                pltpu.VMEM(parent_kv.shape, BF16),
                pltpu.SemaphoreType.DMA((2,)),
            ],
            compiler_params=limit(2),
            name="shard",
        )(*in_hbm(prompt_kv, parent_kv))
        batches, offsets = gather_shards(shard, both, n)
    else:
        rows = 2 * (seg_rows + prompt_rows)
        send = pl.pallas_call(
            pack_kernel,
            out_shape=jax.ShapeDtypeStruct((n, rows, width), BF16),
            in_specs=[SMEM, VMEM, VMEM],
            out_specs=VMEM,
            scratch_shapes=[pltpu.VMEM((parents, rows, width), BF16)],
            name="pack",
        )(fork_list, prompt_kv, parent_kv)
        batches, offsets = [[], [lax.all_to_all(send, "ctx", split_axis=0, concat_axis=0, tiled=True)]], None
    batches = [[s.reshape(-1, rows, width) for s in batch] for batch in batches]
    sizes = [sum(s.shape[0] for s in batch) for batch in batches]
    counts = [sizes[0], sum(sizes[1:])]
    slots = seg_rows + 2 * prompt_rows
    heads = child_q.shape[2] // HD
    masks = []
    for k, count in enumerate(counts):
        if count:
            ahead = 0 if k else span
            masks += [((16, ahead + count * slots), BF16), ((count * slots, HD), F32)]
    query, own, choice, *marks = pl.pallas_call(
        functools.partial(load_kernel, (seg_rows, prompt_rows, sizes, offsets)),
        out_shape=[
            jax.ShapeDtypeStruct(child_q.shape, BF16),
            jax.ShapeDtypeStruct((2, span, width), BF16),
            jax.ShapeDtypeStruct((parents if gather else 1, 8, HD), F32),
            *[jax.ShapeDtypeStruct(*mask) for mask in masks],
        ],
        in_specs=[HBM] * 5,
        out_specs=[VMEM] * (3 + len(masks)),
        scratch_shapes=[
            pltpu.VMEM(child_kv.shape[1:], BF16),
            *[pltpu.SMEM(x.shape, jnp.int32) for x in (fork_list, owner_map, lengths)],
            pltpu.SemaphoreType.DMA((4 + LOADS,)),
        ],
        compiler_params=limit(8),
        name="load",
    )(*in_hbm(fork_list, owner_map, lengths, child_kv[0], child_q))
    marks = [marks[2 * k : 2 * k + 2] for k in range(len(marks) // 2)]
    marks = [[]] * (len(counts) - len(marks)) + marks
    state_shape = jax.ShapeDtypeStruct((HD + 16, heads * span), F32)
    state, fill = pl.pallas_call(
        functools.partial(near_kernel, seg_rows, prompt_rows),
        out_shape=[state_shape, jax.ShapeDtypeStruct((kv_heads, 8, HD), F32)],
        in_specs=[VMEM] * (3 + len(marks[0]) + len(batches[0])),
        out_specs=[VMEM] * 2,
        compiler_params=limit(16),
        name="near",
    )(query, own, choice, *marks[0], *batches[0])
    made = []
    for k in range(1, len(batches) - 1):
        made += pl.pallas_call(
            functools.partial(ready_kernel, seg_rows, prompt_rows, sum(sizes[1:k]) * slots),
            out_shape=[jax.ShapeDtypeStruct((kv_heads, sizes[k] * slots, m * HD), BF16) for m in (2, 1)],
            in_specs=[VMEM] * (3 + len(batches[k])),
            out_specs=[VMEM] * 2,
            compiler_params=limit(4),
        )(choice, fill, marks[1][1], *batches[k])
    last = batches[-1]
    return pl.pallas_call(
        functools.partial(join_kernel, seg_rows, prompt_rows, len(last)),
        out_shape=jax.ShapeDtypeStruct(child_q.shape, BF16),
        in_specs=[VMEM] * (6 + len(last) + len(made)),
        out_specs=HBM,
        scratch_shapes=[pltpu.VMEM(child_q.shape[1:], BF16), pltpu.SemaphoreType.DMA((heads // OUT_HEADS,))],
        compiler_params=limit(16 if gather else 48),
        name="join",
    )(query, choice, fill, state, *marks[1], *last, *made)


def solution(mesh):
    placed = (
        P(("groups", "ctx"), None, None),
        P(("groups", "ctx"), None, None, None),
        P(("groups", "ctx"), None, None),
        P(("groups", "ctx"), None, None, None),
        P("groups"),
        P("groups", None),
        P("groups"),
    )
    return jax.shard_map(
        body,
        mesh=mesh,
        in_specs=placed,
        out_specs=P(("groups", "ctx"), None, None),
        check_vma=False,
    )
```
